256 devices in a mesh: sy: 8 (over z), sx: 32 (over y, x, core).
Axes of the slice: x: 4, y: 4, z: 8, core: 2. Of those that a mesh axis runs over, the one named last changes fastest.
Arguments:
- sky_image: float32 [2048, 4096], P('sy', 'sx'), may hold values from -6 to 6
- observed: float32 [2048, 4096], P('sy', 'sx'), may hold values from -6 to 6
- noise_weight: float32 [2048, 4096], P('sy', 'sx'), may hold values from 0.25 to 4
- basis_tiles: bfloat16 [1024, 128, 128], P(('sy', 'sx')), may hold values from -3 to 3
- intersection: int32 [16, 32, 4], replicated, may hold values from 0 to 1023, as said below
- counts: int32 [16, 32], P('sy', 'sx'), may hold values from 1 to 4
- transfer: float32 [4, 2, 2048, 4096], P(None, None, ('sy', 'sx')), may hold values from -6 to 6
Outputs:
- residual: float32 [2048, 4096], P('sy', 'sx')
- gradient: float32 [2048, 4096], P('sy', 'sx')
The draws below stay inside these ranges and needn't reach their ends.
Inputs may be any that keep to these rules, and one draw needn't show every extreme that they name: `intersection`: every entry names a basis tile held by a device with the same sy index as the sky tile. Of the 8 entries of one device's sky tiles, at most 2 name tiles held by any one device, and in every draw each device reaches 2 at one holder.
All inputs are finite; a program needn't handle non-finite values.
Results may differ from the reference program's by a relative error of at most 0.00045.
Values may be sent and summed in bfloat16 or wider, within the bound.
No kernel may reach another device: no remote copies, remote signals or barrier semaphores. Data moves between devices by JAX's collectives and lax.ppermute only.
A program may use at most 128 MiB of HBM per device.

```python
import math
import jax
import jax.numpy as jnp

K = 4
TILE = 128
ROWS_DEV = 256
COLS_DEV = 128
POOL_DEV = 4
NY = 2048
NX = 4096
TILES_Y = 16
TILES_X = 32
POOL = 1024


def draw_intersection(key, part):
    tiles_down = ROWS_DEV // TILE
    tiles_across = COLS_DEV // TILE
    band_size = TILES_X // tiles_across
    groups_down = TILES_Y // tiles_down
    tile_row = jnp.arange(TILES_Y, dtype=jnp.int32)[:, None, None]
    tile_column = jnp.arange(TILES_X, dtype=jnp.int32)[None, :, None]
    component = jnp.arange(K, dtype=jnp.int32)[None, None, :]
    position = (tile_row % tiles_down * tiles_across + tile_column % tiles_across) * K + component
    shifts = jax.random.randint(jax.random.fold_in(key, 11), (groups_down, band_size), 0, band_size, dtype=jnp.int32)
    shift_here = shifts[tile_row // tiles_down, tile_column // tiles_across]
    holder = (jnp.maximum(position, 1) + shift_here) % band_size
    local_tile = jax.random.randint(jax.random.fold_in(key, 12), (TILES_Y, TILES_X, K), 0, POOL_DEV, dtype=jnp.int32)
    return (tile_row // tiles_down * band_size + holder) * POOL_DEV + local_tile


def place_ends(drawn, rng, least, top_value):
    extent = drawn.shape
    spot = [jax.random.randint(jax.random.fold_in(rng, axis), (), 0, extent[axis]) for axis in range(len(extent))]
    drawn = drawn.at[tuple(spot)].set(least)
    longest = extent.index(max(extent))
    spot[longest] = (spot[longest] + 1) % extent[longest]
    return drawn.at[tuple(spot)].set(top_value)


def block_scale(stream_key, dims, shards, low, high):
    loudness, own = 1.0, jax.random.fold_in(stream_key, 6)
    for dim, parts in shards:
        heights = jnp.exp(jax.random.uniform(jax.random.fold_in(own, dim), (parts,), jnp.float32, low / len(shards), high / len(shards)))
        loudness = loudness * jnp.repeat(heights, dims[dim] // parts).reshape([-1 if axis == dim else 1 for axis in range(len(dims))])
    return loudness


def normal_values(own_key, extent, scale, reach, pieces=(), kind=jnp.bfloat16):
    entries = jax.random.normal(own_key, extent, jnp.float32) * scale
    if len(pieces) > 0:
        entries = block_scale(own_key, extent, pieces, -0.22, 0.18) * entries
    return jnp.clip(entries, min=-reach, max=reach).astype(kind)


def setup_inputs(seed: int = 0) -> dict:
    arg_keys = jax.random.split(jax.random.key(seed), 8)
    return {
        "sky_image": normal_values(arg_keys[0], (NY, NX), 1.0, 6.0, ((0, 8), (1, 32)), jnp.float32),
        "observed": normal_values(arg_keys[1], (NY, NX), 1.0, 6.0, ((0, 8), (1, 32)), jnp.float32),
        "noise_weight": jnp.clip(jnp.exp(math.log(4.0) - 2.7725887 * jax.random.uniform(arg_keys[2], (NY, NX), jnp.float32) ** block_scale(arg_keys[2], (NY, NX), ((0, 8), (1, 32)), -0.2, 0.2)), 0.25, 4.0),
        "basis_tiles": normal_values(arg_keys[3], (POOL, TILE, TILE), 0.5, 3.0, ((0, 256),)),
        "intersection": draw_intersection(jax.random.fold_in(arg_keys[7], 71), 0),
        "counts": place_ends(jax.random.randint(arg_keys[5], (TILES_Y, TILES_X), 1, K + 1), jax.random.fold_in(arg_keys[5], 1), 1, K).astype(jnp.int32),
        "transfer": normal_values(arg_keys[6], (K, 2, NY, NX), 1.0, 6.0, ((2, 256),), jnp.float32),
    }


tv_weight = 0.5
smoothing = 0.25

def coefficient_maps(basis_tiles, intersection, counts):
    collected = []
    for component in range(K):
        picked = basis_tiles[intersection[:, :, component]].astype(jnp.float32)
        in_use = (counts > component).astype(jnp.float32)
        picked = picked * in_use[:, :, None, None]
        collected.append(picked.transpose(0, 2, 1, 3).reshape(NY, NX))
    return collected

def total_variation(field):
    step_x = jnp.roll(field, -1, axis=1) - field
    step_y = jnp.roll(field, -1, axis=0) - field
    magnitude = jnp.sqrt(step_x * step_x + step_y * step_y + smoothing)
    flow_x = step_x / magnitude
    flow_y = step_y / magnitude
    spread = flow_x - jnp.roll(flow_x, 1, axis=1) + flow_y - jnp.roll(flow_y, 1, axis=0)
    return -spread

def reference(sky_image, observed, noise_weight, basis_tiles, intersection, counts, transfer):
    coef_maps = coefficient_maps(basis_tiles, intersection, counts)
    shuffled = transfer.reshape(K, 2, NY // 128, 128, NX // 128, 128)
    shuffled = shuffled.transpose(0, 1, 3, 2, 5, 4).reshape(K, 2, NY, NX)
    model_sum = 0.0
    for component in range(K):
        response = shuffled[component, 0] + 1j * shuffled[component, 1]
        model_sum = model_sum + jnp.fft.fft2(coef_maps[component] * sky_image) * response
    blurred = jnp.real(jnp.fft.ifft2(model_sum))
    residual = noise_weight * (blurred - observed)
    back_spectrum = jnp.fft.fft2(residual)
    data_grad = 0.0
    for component in range(K):
        response = shuffled[component, 0] + 1j * shuffled[component, 1]
        pulled = jnp.real(jnp.fft.ifft2(back_spectrum * jnp.conj(response)))
        data_grad = data_grad + coef_maps[component] * pulled
    gradient = data_grad + tv_weight * total_variation(sky_image)
    return (residual, gradient)
```

```python
import math

import jax
import jax.numpy as jnp
import numpy as np
from jax import lax
from jax.experimental import pallas as pl
from jax.experimental.pallas import tpu as pltpu
from jax.sharding import PartitionSpec as P

highest = lax.Precision.HIGHEST
tv_weight = 0.5
smoothing = 0.25
f32 = jnp.float32
SHORT, LANES, ROWS, PIECE = 32, 128, 8, 16
DEVICES = 256
NX, NY = 4096, 2048
EVERY = ("sy", "sx")


def table(array):
    return np.asarray(array, np.float32)


def circle(left, right, length):
    angles = np.outer(np.arange(left), np.arange(right)) % length * (2.0 * np.pi / length)
    return np.cos(angles), np.sin(angles)


def joined(cos, sin, sign):
    return table(np.block([[cos, sign * sin], [-sign * sin, cos]]))


def make_tables():
    cos_turn, sin_turn = circle(SHORT, LANES, NX)
    cos_long, sin_long = circle(LANES, LANES, LANES)
    cos_dev, sin_dev = circle(DEVICES, DEVICES, DEVICES)
    cos_row, sin_row = circle(DEVICES, ROWS, NY)
    cos_eight, sin_eight = circle(ROWS, ROWS, ROWS)
    spread = np.eye(PIECE)
    wide = lambda matrix: np.kron(matrix, spread)
    lane = np.arange(LANES)
    kappa = np.arange(DEVICES)
    flip = np.zeros((LANES, LANES))
    flip[LANES - 1 - lane, lane] = 1.0
    flip_first = np.zeros((LANES, LANES))
    flip_first[(LANES - lane) % LANES, lane] = 1.0
    flip_rows = np.zeros((DEVICES, DEVICES))
    flip_rows[kappa, (DEVICES - kappa) % DEVICES] = 1.0
    lam = np.arange(ROWS)
    flip_lam = np.zeros((ROWS, ROWS))
    flip_lam[ROWS - 1 - lam, lam] = 1.0
    flip_lam_first = np.zeros((ROWS, ROWS))
    flip_lam_first[(ROWS - lam) % ROWS, lam] = 1.0
    return dict(
        turn_x=table(np.stack([cos_turn, sin_turn])),
        x_forward=joined(cos_long, sin_long, -1.0),
        x_inverse=joined(cos_long, sin_long, 1.0),
        y_long=table(np.concatenate([cos_dev, sin_dev])),
        turn_y=table(
            np.stack([np.repeat(cos_row, PIECE, axis=1), np.repeat(sin_row, PIECE, axis=1)])
        ),
        y_forward=joined(wide(cos_eight), wide(sin_eight), -1.0),
        y_inverse=joined(wide(cos_eight), wide(sin_eight), 1.0),
        flips=table(np.stack([flip, flip_first])),
        flip_rows=table(flip_rows),
        flip_lams=table(np.stack([wide(flip_lam), wide(flip_lam_first)])),
    )


def dot(left, right):
    return jnp.dot(left, right, precision=highest, preferred_element_type=f32)


def run(body, shapes, *operands, scalars=0, scratch=()):
    whole = pl.BlockSpec(memory_space=pltpu.VMEM)
    single = not isinstance(shapes, (list, tuple))
    return pl.pallas_call(
        body,
        out_shape=shapes,
        in_specs=[pl.BlockSpec(memory_space=pltpu.SMEM)] * scalars
        + [whole] * (len(operands) - scalars),
        out_specs=whole if single else [whole] * len(shapes),
        scratch_shapes=list(scratch),
        compiler_params=pltpu.CompilerParams(vmem_limit_bytes=48 * 1024 * 1024),
    )(*operands)


def shaped(*dims, dtype=f32):
    return jax.ShapeDtypeStruct(dims, dtype)


def swap_blocks(field):
    sub = lax.broadcasted_iota(jnp.int32, field.shape, 1)
    group = lax.broadcasted_iota(jnp.int32, field.shape, 2) // PIECE
    for step in (1, 2, 4):
        low = (sub & step) == 0
        shift = PIECE * step
        if step == 4:
            other = pltpu.roll(pltpu.roll(field, shift, 2), step, 1)
        else:
            moved = jnp.where(
                low, pltpu.roll(field, LANES - shift, 2), pltpu.roll(field, shift, 2)
            )
            other = jnp.where(
                low, pltpu.roll(moved, ROWS - step, 1), pltpu.roll(moved, step, 1)
            )
        field = jnp.where(low == ((group & step) == 0), field, other)
    return field


def add(left, right):
    if left is None or right is None:
        return right if left is None else left
    return left + right


def subtract(left, right):
    if right is None:
        return left
    return -right if left is None else left - right


def scaled(value, factor):
    return None if value is None else value * f32(factor)


def turned(real, imag, cos, sin):
    return (
        subtract(scaled(real, cos), scaled(imag, sin)),
        add(scaled(real, sin), scaled(imag, cos)),
    )


def short_transform(points, sign):
    length = len(points)
    if length == 1:
        return points
    even = short_transform(points[0::2], sign)
    odd = short_transform(points[1::2], sign)
    low, high = [], []
    for k in range(length // 2):
        real, imag = odd[k]
        if k == 0:
            part = (real, imag)
        elif 4 * k == length:
            part = (
                (None if imag is None else imag * f32(-sign)),
                (None if real is None else real * f32(sign)),
            )
        else:
            angle = 2.0 * math.pi * k / length
            part = turned(real, imag, math.cos(angle), sign * math.sin(angle))
        low.append((add(even[k][0], part[0]), add(even[k][1], part[1])))
        high.append((subtract(even[k][0], part[0]), subtract(even[k][1], part[1])))
    return low + high


def rows_to_lines(points, turn, matrix, work):
    for c, (real, imag) in enumerate(short_transform(points, -1.0)):
        cos, sin = turn[0, c : c + 1, :], turn[1, c : c + 1, :]
        imag = jnp.zeros_like(real) if imag is None else imag
        work[ROWS * c : ROWS * (c + 1), :LANES] = real * cos + imag * sin
        work[ROWS * c : ROWS * (c + 1), LANES:] = imag * cos - real * sin
    lines = dot(work[...], matrix[...])
    return [
        swap_blocks(part.reshape(SHORT, ROWS, LANES)).reshape(DEVICES, LANES)
        for part in (lines[:, :LANES], lines[:, LANES:])
    ]


def lines_to_rows(real, imag, turn, matrix, work):
    parts = [
        swap_blocks(part.reshape(SHORT, ROWS, LANES)).reshape(DEVICES, LANES)
        for part in (real, imag)
    ]
    work[...] = dot(jnp.concatenate(parts, axis=1), matrix[...])
    points = []
    for c in range(SHORT):
        cos, sin = turn[0, c : c + 1, :], turn[1, c : c + 1, :]
        real = work[ROWS * c : ROWS * (c + 1), :LANES]
        imag = work[ROWS * c : ROWS * (c + 1), LANES:]
        points.append((real * cos - imag * sin, real * sin + imag * cos))
    return short_transform(points, 1.0)


def forward_y(received, fields, y_long, turn_y, matrix):
    stacked = jnp.concatenate(
        [received[pl.ds(f, DEVICES, stride=fields), :] for f in range(fields)], axis=1
    )
    both = dot(y_long[...], stacked)
    by_cos, by_sin = both[:DEVICES], both[DEVICES:]
    cos, sin = turn_y[0], turn_y[1]
    spectra = []
    for f in range(0, fields, 2):
        at_real = slice(f * LANES, (f + 1) * LANES)
        at_imag = slice((f + 1) * LANES, (f + 2) * LANES)
        real = by_cos[:, at_real] + by_sin[:, at_imag]
        imag = by_cos[:, at_imag] - by_sin[:, at_real]
        lines = jnp.concatenate([real * cos + imag * sin, imag * cos - real * sin], axis=1)
        out = dot(lines, matrix[...])
        spectra.append((out[:, :LANES], out[:, LANES:]))
    return spectra


def inverse_y(spectra, y_long, turn_y, matrix, sent):
    cos, sin = turn_y[0], turn_y[1]
    columns = []
    for real, imag in spectra:
        lines = dot(jnp.concatenate([real, imag], axis=1), matrix[...])
        real, imag = lines[:, :LANES], lines[:, LANES:]
        columns += [real * cos - imag * sin, real * sin + imag * cos]
    fields = len(columns)
    both = dot(y_long[...], jnp.concatenate(columns, axis=1))
    by_cos, by_sin = both[:DEVICES], both[DEVICES:]
    for f in range(0, fields, 2):
        at_real = slice(f * LANES, (f + 1) * LANES)
        at_imag = slice((f + 1) * LANES, (f + 2) * LANES)
        sent[pl.ds(f, DEVICES, stride=fields), :] = by_cos[:, at_real] - by_sin[:, at_imag]
        sent[pl.ds(f + 1, DEVICES, stride=fields), :] = by_cos[:, at_imag] + by_sin[:, at_real]


def pack_tiles(tiles, sent):
    for piece in range(PIECE):
        rows = jnp.concatenate(
            [
                tiles[l, ROWS * piece : ROWS * (piece + 1), :].astype(f32)
                for l in range(tiles.shape[0])
            ],
            axis=0,
        ).astype(jnp.bfloat16)
        sent[piece] = rows
        sent[piece + PIECE] = rows


def pack_pixels(counts, sky, observed, noise, sent):
    lane = lax.broadcasted_iota(jnp.int32, (ROWS, LANES), 1)
    for r in range(SHORT):
        rows = slice(ROWS * r, ROWS * (r + 1))
        sent[r, 0:ROWS, :] = sky[rows, :]
        sent[r, ROWS : 2 * ROWS, :] = observed[rows, :]
        used = lane < counts[r // PIECE]
        weight = noise[rows, :]
        sent[r, 2 * ROWS :, :] = jnp.where(used, -weight, weight)


def first_rows(wanted, tiles, pixels, turn, matrix, sent, coef, pool, work):
    pool[...] = tiles[...].astype(f32)
    for p in range(2):
        points = []
        for b in range(SHORT):
            sky = pixels[b, 0:ROWS, :]
            weight = pixels[b, 2 * ROWS :, :]
            pair = []
            for k in (2 * p, 2 * p + 1):
                start = pl.multiple_of(wanted[4 * b + k] * ROWS, ROWS)
                mask = jnp.where(weight[:, k : k + 1] < 0.0, f32(1.0), f32(0.0))
                value = pool[pl.ds(start, ROWS), :] * mask
                coef[k, b] = value
                pair.append(value * sky)
            points.append(tuple(pair))
        real, imag = rows_to_lines(points, turn, matrix, work)
        sent[pl.ds(2 * p, DEVICES, stride=4), :] = real
        sent[pl.ds(2 * p + 1, DEVICES, stride=4), :] = imag


def middle_lines(received, response, y_long, turn_y, forward, inverse, sent):
    spectra = forward_y(received, 4, y_long, turn_y, forward)
    real = imag = 0.0
    for p, (z_real, z_imag) in enumerate(spectra):
        c_real, c_imag = response[2 * p], response[2 * p + 1]
        real = real + z_real * c_real - z_imag * c_imag
        imag = imag + z_real * c_imag + z_imag * c_real
    inverse_y([(real, imag)], y_long, turn_y, inverse, sent)


def middle_rows(received, pixels, turn, forward, inverse, sent, residual, work):
    points = lines_to_rows(
        received[pl.ds(0, DEVICES, stride=2), :],
        received[pl.ds(1, DEVICES, stride=2), :],
        turn,
        inverse,
        work,
    )
    values = []
    for b in range(SHORT):
        weight = jnp.abs(pixels[b, 2 * ROWS :, :])
        value = weight * (points[b][0] - pixels[b, ROWS : 2 * ROWS, :])
        residual[b] = value
        values.append((value, None))
    real, imag = rows_to_lines(values, turn, forward, work)
    sent[pl.ds(0, DEVICES, stride=2), :] = real
    sent[pl.ds(1, DEVICES, stride=2), :] = imag


def last_lines(received, response, y_long, turn_y, forward, inverse, sent):
    ((real, imag),) = forward_y(received, 2, y_long, turn_y, forward)
    spectra = []
    for p in range(2):
        c_real, c_imag = response[2 * p], response[2 * p + 1]
        spectra.append((real * c_real + imag * c_imag, imag * c_real - real * c_imag))
    inverse_y(spectra, y_long, turn_y, inverse, sent)


def last_rows(received, coef, residual, flow, turn, inverse, sent, work):
    total = None
    for p in range(2):
        points = lines_to_rows(
            received[pl.ds(2 * p, DEVICES, stride=4), :],
            received[pl.ds(2 * p + 1, DEVICES, stride=4), :],
            turn,
            inverse,
            work,
        )
        for b in range(SHORT):
            value = coef[2 * p, b] * points[b][0] + coef[2 * p + 1, b] * points[b][1]
            if p == 0:
                sent[b, 0:ROWS, :] = value + flow[b]
            else:
                sent[b, 0:ROWS, :] += value
    for b in range(SHORT):
        sent[b, ROWS:, :] = residual[b]


def variation(pixels, above, below, flow):
    sky = pixels[:, 0:ROWS, :]
    lane = lax.broadcasted_iota(jnp.int32, sky.shape, 2)
    sub = lax.broadcasted_iota(jnp.int32, sky.shape, 1)

    def after(field):
        moved = pltpu.roll(field, LANES - 1, 2)
        following = jnp.concatenate([moved[1:], moved[:1]], axis=0)
        return jnp.where(lane == LANES - 1, following, moved)

    def flows(field, following):
        step_x = after(field) - field
        step_y = following - field
        magnitude = jnp.sqrt(step_x * step_x + step_y * step_y + smoothing)
        return step_x / magnitude, step_y / magnitude

    upper = jnp.broadcast_to(above[...].reshape(SHORT, 1, LANES), sky.shape)
    lower = jnp.broadcast_to(below[...].reshape(SHORT, 1, LANES), sky.shape)
    following = jnp.where(sub == ROWS - 1, lower, pltpu.roll(sky, ROWS - 1, 1))
    flow_x, flow_y = flows(sky, following)
    _, upper_y = flows(upper, sky)
    moved = pltpu.roll(flow_x, 1, 2)
    before_x = jnp.where(
        lane == 0, jnp.concatenate([moved[-1:], moved[:-1]], axis=0), moved
    )
    before_y = jnp.where(sub == 0, upper_y, pltpu.roll(flow_y, 1, 1))
    flow[...] = -tv_weight * (flow_x - before_x + flow_y - before_y)


def pack_transfer(transfer, flips, sent, mirrored):
    for p in range(2):
        for c in range(SHORT):
            at = slice(LANES * c, LANES * (c + 1))
            real_1, imag_1 = transfer[2 * p, 0, :, at], transfer[2 * p, 1, :, at]
            real_2, imag_2 = transfer[2 * p + 1, 0, :, at], transfer[2 * p + 1, 1, :, at]
            rows = slice(ROWS * c, ROWS * (c + 1))
            mirrored[2 * p, rows, :] = real_1 - imag_2
            mirrored[2 * p + 1, rows, :] = imag_1 + real_2
            mirrored[4 + 2 * p, rows, :] = real_1 + imag_2
            mirrored[5 + 2 * p, rows, :] = imag_1 - real_2
    for f in range(4):
        field = mirrored[4 + f].reshape(SHORT, ROWS, LANES)
        sent[pl.ds(f, DEVICES, stride=8), :] = swap_blocks(field).reshape(DEVICES, LANES)
        first = dot(mirrored[f, 0:ROWS, :], flips[1])
        others = dot(mirrored[f], flips[0])
        blocks = [first] + [others[ROWS * c : ROWS * (c + 1)] for c in range(SHORT - 1, 0, -1)]
        field = jnp.stack(blocks)
        sent[pl.ds(4 + f, DEVICES, stride=8), :] = swap_blocks(field).reshape(DEVICES, LANES)


def make_response(received, flip_rows, flip_lams, response, fields):
    def place(v, carry):
        for low in range(2):
            for f in range(8):
                block = received[pl.ds((PIECE * v + low) * 8 + f, ROWS, stride=16), :]
                block = swap_blocks(block.reshape(1, ROWS, LANES)).reshape(ROWS, LANES)
                fields[f, pl.ds(LANES * low + v, ROWS, stride=PIECE), :] = block
        return carry

    lax.fori_loop(0, PIECE, place, 0)
    scale = f32(0.5 / (NX * NY))
    top = lax.broadcasted_iota(jnp.int32, (DEVICES, LANES), 0) == 0
    for f in range(4):
        swapped = dot(flip_rows[...], fields[4 + f])
        mirror = dot(swapped, flip_lams[0])
        first = dot(swapped[0:ROWS], flip_lams[1])
        mirror = jnp.where(top, jnp.broadcast_to(first[0:1], mirror.shape), mirror)
        if f % 2 == 0:
            response[f] = (fields[f] + mirror) * scale
        else:
            response[f] = (fields[f] - mirror) * scale


def exchange(sent, axis, count):
    pieces = sent.reshape(count, sent.size // count // LANES, LANES)
    return lax.all_to_all(pieces, axis, split_axis=0, concat_axis=0, tiled=True).reshape(
        sent.shape
    )


def on_device(sky_image, observed, noise_weight, basis_tiles, intersection, counts, transfer):
    tables = {name: jnp.asarray(value) for name, value in make_tables().items()}
    band, column = lax.axis_index("sy"), lax.axis_index("sx")
    zero = jnp.zeros((), jnp.int32)
    wanted = lax.dynamic_slice(
        intersection, (2 * band + column // PIECE, zero, zero), (1, SHORT, 4)
    ).reshape(SHORT * 4) - band * LANES

    tiles = exchange(
        run(pack_tiles, shaped(SHORT, SHORT, LANES, dtype=jnp.bfloat16), basis_tiles), "sx", SHORT
    )
    pixels = exchange(
        run(
            pack_pixels,
            shaped(SHORT, 3 * ROWS, LANES),
            counts.reshape(2),
            sky_image,
            observed,
            noise_weight,
            scalars=1,
        ),
        "sx",
        SHORT,
    )
    spread = exchange(
        run(
            pack_transfer,
            shaped(DEVICES * 8, LANES),
            transfer,
            tables["flips"],
            scratch=[pltpu.VMEM((8, DEVICES, LANES), f32)],
        ),
        EVERY,
        DEVICES,
    )
    work = [pltpu.VMEM((DEVICES, 2 * LANES), f32)]
    sent, coef = run(
        first_rows,
        [shaped(DEVICES * 4, LANES), shaped(4, SHORT, ROWS, LANES)],
        wanted,
        tiles.reshape(SHORT * SHORT, LANES),
        pixels,
        tables["turn_x"],
        tables["x_forward"],
        scalars=1,
        scratch=[pltpu.VMEM((SHORT * SHORT, LANES), f32)] + work,
    )
    received = exchange(sent, EVERY, DEVICES)

    ahead = [(i, (i + 1) % DEVICES) for i in range(DEVICES)]
    behind = [(target, source) for source, target in ahead]
    above = lax.ppermute(pixels[:, ROWS - 1, :], EVERY, ahead)
    below = lax.ppermute(pixels[:, 0, :], EVERY, behind)
    flow = run(variation, shaped(SHORT, ROWS, LANES), pixels, above, below)
    response = run(
        make_response,
        shaped(4, DEVICES, LANES),
        spread,
        tables["flip_rows"],
        tables["flip_lams"],
        scratch=[pltpu.VMEM((8, DEVICES, LANES), f32)],
    )
    y_tables = [tables[name] for name in ("y_long", "turn_y", "y_forward", "y_inverse")]
    x_tables = [tables[name] for name in ("turn_x", "x_forward", "x_inverse")]
    sent = run(middle_lines, shaped(DEVICES * 2, LANES), received, response, *y_tables)
    received = exchange(sent, EVERY, DEVICES)
    sent, residual = run(
        middle_rows,
        [shaped(DEVICES * 2, LANES), shaped(SHORT, ROWS, LANES)],
        received,
        pixels,
        *x_tables,
        scratch=work,
    )
    received = exchange(sent, EVERY, DEVICES)
    sent = run(last_lines, shaped(DEVICES * 4, LANES), received, response, *y_tables)
    received = exchange(sent, EVERY, DEVICES)
    sent = run(
        last_rows,
        shaped(SHORT, 2 * ROWS, LANES),
        received,
        coef,
        residual,
        flow,
        tables["turn_x"],
        tables["x_inverse"],
        scratch=work,
    )
    blocks = exchange(sent, "sx", SHORT)
    gradient = blocks[:, :ROWS, :].reshape(SHORT * ROWS, LANES)
    residual = blocks[:, ROWS:, :].reshape(SHORT * ROWS, LANES)
    return (residual, gradient)


def solution(mesh):
    placed = (
        P("sy", "sx"),
        P("sy", "sx"),
        P("sy", "sx"),
        P(("sy", "sx"), None, None),
        P(),
        P("sy", "sx"),
        P(None, None, ("sy", "sx"), None),
    )
    return jax.shard_map(
        on_device,
        mesh=mesh,
        in_specs=placed,
        out_specs=(P("sy", "sx"), P("sy", "sx")),
        check_vma=False,
    )
```

```python
import math

import jax
import jax.numpy as jnp
import numpy as np
from jax import lax
from jax.experimental import pallas as pl
from jax.experimental.pallas import tpu as pltpu
from jax.sharding import PartitionSpec as P

highest = lax.Precision.HIGHEST
tv_weight = 0.5
smoothing = 0.25
f32 = jnp.float32
SHORT, LANES, ROWS, PIECE = 32, 128, 8, 16
DEVICES = 256
TILE_ROWS = 32
CODE_BITS = 13
NX, NY = 4096, 2048
EVERY = ("sy", "sx")


def table(array):
    return np.asarray(array, np.float32)


def circle(left, right, length):
    angles = np.outer(np.arange(left), np.arange(right)) % length * (2.0 * np.pi / length)
    return np.cos(angles), np.sin(angles)


def joined(cos, sin, sign):
    return table(np.block([[cos, sign * sin], [-sign * sin, cos]]))


def make_tables():
    cos_turn, sin_turn = circle(SHORT, LANES, NX)
    cos_long, sin_long = circle(LANES, LANES, LANES)
    cos_dev, sin_dev = circle(DEVICES, DEVICES, DEVICES)
    cos_row, sin_row = circle(DEVICES, ROWS, NY)
    cos_eight, sin_eight = circle(ROWS, ROWS, ROWS)
    spread = np.eye(PIECE)
    wide = lambda matrix: np.kron(matrix, spread)
    lane = np.arange(LANES)
    kappa = np.arange(DEVICES)
    flip = np.zeros((LANES, LANES))
    flip[LANES - 1 - lane, lane] = 1.0
    flip_first = np.zeros((LANES, LANES))
    flip_first[(LANES - lane) % LANES, lane] = 1.0
    flip_rows = np.zeros((DEVICES, DEVICES))
    flip_rows[kappa, (DEVICES - kappa) % DEVICES] = 1.0
    lam = np.arange(ROWS)
    flip_lam = np.zeros((ROWS, ROWS))
    flip_lam[ROWS - 1 - lam, lam] = 1.0
    flip_lam_first = np.zeros((ROWS, ROWS))
    flip_lam_first[(ROWS - lam) % ROWS, lam] = 1.0
    return dict(
        turn_x=table(np.stack([cos_turn, sin_turn])),
        x_forward=joined(cos_long, sin_long, -1.0),
        x_inverse=joined(cos_long, sin_long, 1.0),
        y_long=table(np.concatenate([cos_dev, sin_dev])),
        turn_y=table(
            np.stack([np.repeat(cos_row, PIECE, axis=1), np.repeat(sin_row, PIECE, axis=1)])
        ),
        y_forward=joined(wide(cos_eight), wide(sin_eight), -1.0),
        y_inverse=joined(wide(cos_eight), wide(sin_eight), 1.0),
        flips=table(np.stack([flip, flip_first])),
        flip_rows=table(flip_rows),
        flip_lams=table(np.stack([wide(flip_lam), wide(flip_lam_first)])),
    )


def dot(left, right):
    return jnp.dot(left, right, precision=highest, preferred_element_type=f32)


def run(body, shapes, *operands, scalars=0, scratch=()):
    whole = pl.BlockSpec(memory_space=pltpu.VMEM)
    single = not isinstance(shapes, (list, tuple))
    return pl.pallas_call(
        body,
        out_shape=shapes,
        in_specs=[pl.BlockSpec(memory_space=pltpu.SMEM)] * scalars
        + [whole] * (len(operands) - scalars),
        out_specs=whole if single else [whole] * len(shapes),
        scratch_shapes=list(scratch),
        compiler_params=pltpu.CompilerParams(vmem_limit_bytes=48 * 1024 * 1024),
    )(*operands)


def shaped(*dims, dtype=f32):
    return jax.ShapeDtypeStruct(dims, dtype)


def swap_blocks(field):
    sub = lax.broadcasted_iota(jnp.int32, field.shape, 1)
    group = lax.broadcasted_iota(jnp.int32, field.shape, 2) // PIECE
    for step in (1, 2, 4):
        low = (sub & step) == 0
        shift = PIECE * step
        if step == 4:
            other = pltpu.roll(pltpu.roll(field, shift, 2), step, 1)
        else:
            moved = jnp.where(
                low, pltpu.roll(field, LANES - shift, 2), pltpu.roll(field, shift, 2)
            )
            other = jnp.where(
                low, pltpu.roll(moved, ROWS - step, 1), pltpu.roll(moved, step, 1)
            )
        field = jnp.where(low == ((group & step) == 0), field, other)
    return field


def add(left, right):
    if left is None or right is None:
        return right if left is None else left
    return left + right


def subtract(left, right):
    if right is None:
        return left
    return -right if left is None else left - right


def scaled(value, factor):
    return None if value is None else value * f32(factor)


def turned(real, imag, cos, sin):
    return (
        subtract(scaled(real, cos), scaled(imag, sin)),
        add(scaled(real, sin), scaled(imag, cos)),
    )


def short_transform(points, sign):
    length = len(points)
    if length == 1:
        return points
    even = short_transform(points[0::2], sign)
    odd = short_transform(points[1::2], sign)
    low, high = [], []
    for k in range(length // 2):
        real, imag = odd[k]
        if k == 0:
            part = (real, imag)
        elif 4 * k == length:
            part = (
                (None if imag is None else imag * f32(-sign)),
                (None if real is None else real * f32(sign)),
            )
        else:
            angle = 2.0 * math.pi * k / length
            part = turned(real, imag, math.cos(angle), sign * math.sin(angle))
        low.append((add(even[k][0], part[0]), add(even[k][1], part[1])))
        high.append((subtract(even[k][0], part[0]), subtract(even[k][1], part[1])))
    return low + high


def swapped(field):
    return swap_blocks(field.reshape(SHORT, ROWS, LANES)).reshape(DEVICES, LANES)


def encode(values):
    top = jnp.maximum(
        jnp.maximum(jnp.abs(values[0]), jnp.abs(values[1])),
        jnp.maximum(jnp.abs(values[2]), jnp.abs(values[3])),
    )
    power = jnp.ceil(jnp.log2(jnp.maximum(top, f32(2.0**-100))))
    factor = jnp.exp2(f32(CODE_BITS) - power)
    limit = 2.0**CODE_BITS - 1.0
    codes = [
        jnp.clip(jnp.floor(value * factor + 0.5), -limit, limit).astype(jnp.int32)
        for value in values
    ]
    shared = power.astype(jnp.int32) + 128
    return (
        (codes[0] << 18) | ((codes[1] & 0x3FFF) << 4) | (shared >> 4),
        (codes[2] << 18) | ((codes[3] & 0x3FFF) << 4) | (shared & 15),
    )


def decode(first, second):
    power = (((first & 15) << 4) | (second & 15)) - (128 + CODE_BITS)
    factor = jnp.exp2(power.astype(f32))
    return [
        code.astype(f32) * factor
        for code in (first >> 18, (first << 14) >> 18, second >> 18, (second << 14) >> 18)
    ]


def rows_to_lines(points, turn, matrix, work):
    for c, (real, imag) in enumerate(short_transform(points, -1.0)):
        cos, sin = turn[0, c : c + 1, :], turn[1, c : c + 1, :]
        imag = jnp.zeros_like(real) if imag is None else imag
        work[ROWS * c : ROWS * (c + 1), :LANES] = real * cos + imag * sin
        work[ROWS * c : ROWS * (c + 1), LANES:] = imag * cos - real * sin
    lines = dot(work[...], matrix[...])
    return [lines[:, :LANES], lines[:, LANES:]]


def lines_to_rows(real, imag, turn, matrix, work):
    work[...] = dot(jnp.concatenate([real, imag], axis=1), matrix[...])
    points = []
    for c in range(SHORT):
        cos, sin = turn[0, c : c + 1, :], turn[1, c : c + 1, :]
        real = work[ROWS * c : ROWS * (c + 1), :LANES]
        imag = work[ROWS * c : ROWS * (c + 1), LANES:]
        points.append((real * cos - imag * sin, real * sin + imag * cos))
    return short_transform(points, 1.0)


def forward_y(received, y_long, turn_y, matrix):
    both = dot(y_long[...], jnp.concatenate(received, axis=1))
    by_cos, by_sin = both[:DEVICES], both[DEVICES:]
    cos, sin = turn_y[0], turn_y[1]
    spectra = []
    for f in range(0, len(received), 2):
        at_real = slice(f * LANES, (f + 1) * LANES)
        at_imag = slice((f + 1) * LANES, (f + 2) * LANES)
        real = by_cos[:, at_real] + by_sin[:, at_imag]
        imag = by_cos[:, at_imag] - by_sin[:, at_real]
        lines = jnp.concatenate([real * cos + imag * sin, imag * cos - real * sin], axis=1)
        out = dot(lines, matrix[...])
        spectra.append((out[:, :LANES], out[:, LANES:]))
    return spectra


def inverse_y(spectra, y_long, turn_y, matrix):
    cos, sin = turn_y[0], turn_y[1]
    columns = []
    for real, imag in spectra:
        lines = dot(jnp.concatenate([real, imag], axis=1), matrix[...])
        real, imag = lines[:, :LANES], lines[:, LANES:]
        columns += [real * cos - imag * sin, real * sin + imag * cos]
    both = dot(y_long[...], jnp.concatenate(columns, axis=1))
    by_cos, by_sin = both[:DEVICES], both[DEVICES:]
    fields = []
    for f in range(0, len(columns), 2):
        at_real = slice(f * LANES, (f + 1) * LANES)
        at_imag = slice((f + 1) * LANES, (f + 2) * LANES)
        fields.append(by_cos[:, at_real] - by_sin[:, at_imag])
        fields.append(by_cos[:, at_imag] + by_sin[:, at_real])
    return fields


def every(ref, index, count):
    return ref[pl.ds(index, DEVICES, stride=count), :]


def put(ref, fields, first, count):
    for f, field in enumerate(fields):
        ref[pl.ds(first + f, DEVICES, stride=count), :] = field


def halves(value):
    high = value.astype(jnp.bfloat16).astype(f32)
    return jnp.concatenate([high, value - high], axis=0).astype(jnp.bfloat16)


def pixel(parts, b, field):
    start = TILE_ROWS + 2 * ROWS * field
    both = parts[b, start : start + 2 * ROWS, :].astype(f32)
    return both[:ROWS] + both[ROWS:]


def pack_inputs(counts, tiles, sky, observed, noise, sent):
    for piece in range(PIECE):
        rows = jnp.concatenate(
            [
                tiles[l, ROWS * piece : ROWS * (piece + 1), :].astype(f32)
                for l in range(tiles.shape[0])
            ],
            axis=0,
        ).astype(jnp.bfloat16)
        sent[piece, :TILE_ROWS, :] = rows
        sent[piece + PIECE, :TILE_ROWS, :] = rows
    lane = lax.broadcasted_iota(jnp.int32, (ROWS, LANES), 1)
    for r in range(SHORT):
        rows = slice(ROWS * r, ROWS * (r + 1))
        weight = noise[rows, :]
        weight = jnp.where(lane < counts[r // PIECE], -weight, weight)
        for f, value in enumerate((sky[rows, :], observed[rows, :], weight)):
            start = TILE_ROWS + 2 * ROWS * f
            sent[r, start : start + 2 * ROWS, :] = halves(value)


def first_rows(wanted, parts, spread, turn, matrix, sent, coef, pixels, top, bottom, pool, work):
    for h in range(SHORT):
        pool[TILE_ROWS * h : TILE_ROWS * (h + 1), :] = parts[h, :TILE_ROWS, :].astype(f32)
    fields = []
    for p in range(2):
        points = []
        for b in range(SHORT):
            if p == 0:
                sky = pixel(parts, b, 0)
                pixels[b] = sky
                top[b : b + 1, :] = sky[:1]
                bottom[b : b + 1, :] = sky[ROWS - 1 :]
            sky = pixels[b]
            weight = parts[b, TILE_ROWS + 4 * ROWS : TILE_ROWS + 6 * ROWS, :].astype(f32)[:ROWS]
            pair = []
            for k in (2 * p, 2 * p + 1):
                start = pl.multiple_of(wanted[4 * b + k] * ROWS, ROWS)
                mask = jnp.where(weight[:, k : k + 1] < 0.0, f32(1.0), f32(0.0))
                value = pool[pl.ds(start, ROWS), :] * mask
                coef[k, b] = value
                pair.append(value * sky)
            points.append(tuple(pair))
        fields += rows_to_lines(points, turn, matrix, work)
    put(sent, [swapped(word) for word in encode(fields)], 0, 6)
    put(sent, [spread[word] for word in range(4)], 2, 6)


def middle_lines(
    received, flip_rows, flip_lams, y_long, turn_y, forward, inverse, sent, response, fields
):
    make_response(received, flip_rows, flip_lams, response, fields)
    spectra = forward_y(
        decode(every(received, 0, 6), every(received, 1, 6)), y_long, turn_y, forward
    )
    real = imag = 0.0
    for p, (z_real, z_imag) in enumerate(spectra):
        c_real, c_imag = response[2 * p], response[2 * p + 1]
        real = real + z_real * c_real - z_imag * c_imag
        imag = imag + z_real * c_imag + z_imag * c_real
    put(sent, inverse_y([(real, imag)], y_long, turn_y, inverse), 0, 2)


def middle_rows(received, parts, turn, forward, inverse, sent, residual, work):
    points = lines_to_rows(
        swapped(every(received, 0, 2)), swapped(every(received, 1, 2)), turn, inverse, work
    )
    values = []
    for b in range(SHORT):
        value = jnp.abs(pixel(parts, b, 2)) * (points[b][0] - pixel(parts, b, 1))
        residual[b] = value
        values.append((value, None))
    fields = rows_to_lines(values, turn, forward, work)
    put(sent, [swapped(field) for field in fields], 0, 2)


def last_lines(received, response, y_long, turn_y, forward, inverse, sent):
    ((real, imag),) = forward_y(
        [every(received, 0, 2), every(received, 1, 2)], y_long, turn_y, forward
    )
    spectra = []
    for p in range(2):
        c_real, c_imag = response[2 * p], response[2 * p + 1]
        spectra.append((real * c_real + imag * c_imag, imag * c_real - real * c_imag))
    put(sent, encode(inverse_y(spectra, y_long, turn_y, inverse)), 0, 2)


def last_rows(received, coef, residual, flow, turn, inverse, sent, work):
    fields = decode(swapped(every(received, 0, 2)), swapped(every(received, 1, 2)))
    for p in range(2):
        points = lines_to_rows(fields[2 * p], fields[2 * p + 1], turn, inverse, work)
        for b in range(SHORT):
            value = coef[2 * p, b] * points[b][0] + coef[2 * p + 1, b] * points[b][1]
            if p == 0:
                sent[b, 0:ROWS, :] = value + flow[b]
            else:
                sent[b, 0:ROWS, :] += value
    for b in range(SHORT):
        sent[b, ROWS:, :] = residual[b]


def variation(pixels, above, below, flow):
    sky = pixels[...]
    lane = lax.broadcasted_iota(jnp.int32, sky.shape, 2)
    sub = lax.broadcasted_iota(jnp.int32, sky.shape, 1)

    def after(field):
        moved = pltpu.roll(field, LANES - 1, 2)
        following = jnp.concatenate([moved[1:], moved[:1]], axis=0)
        return jnp.where(lane == LANES - 1, following, moved)

    def flows(field, following):
        step_x = after(field) - field
        step_y = following - field
        magnitude = jnp.sqrt(step_x * step_x + step_y * step_y + smoothing)
        return step_x / magnitude, step_y / magnitude

    upper = jnp.broadcast_to(above[...].reshape(SHORT, 1, LANES), sky.shape)
    lower = jnp.broadcast_to(below[...].reshape(SHORT, 1, LANES), sky.shape)
    following = jnp.where(sub == ROWS - 1, lower, pltpu.roll(sky, ROWS - 1, 1))
    flow_x, flow_y = flows(sky, following)
    _, upper_y = flows(upper, sky)
    moved = pltpu.roll(flow_x, 1, 2)
    before_x = jnp.where(
        lane == 0, jnp.concatenate([moved[-1:], moved[:-1]], axis=0), moved
    )
    before_y = jnp.where(sub == 0, upper_y, pltpu.roll(flow_y, 1, 1))
    flow[...] = -tv_weight * (flow_x - before_x + flow_y - before_y)


def pack_transfer(transfer, flips, sent, mirrored):
    for p in range(2):
        for c in range(SHORT):
            at = slice(LANES * c, LANES * (c + 1))
            real_1, imag_1 = transfer[2 * p, 0, :, at], transfer[2 * p, 1, :, at]
            real_2, imag_2 = transfer[2 * p + 1, 0, :, at], transfer[2 * p + 1, 1, :, at]
            rows = slice(ROWS * c, ROWS * (c + 1))
            mirrored[2 * p, rows, :] = real_1 - imag_2
            mirrored[2 * p + 1, rows, :] = imag_1 + real_2
            mirrored[4 + 2 * p, rows, :] = real_1 + imag_2
            mirrored[5 + 2 * p, rows, :] = imag_1 - real_2
    direct, reverse = [], []
    for f in range(4):
        direct.append(mirrored[4 + f])
        first = dot(mirrored[f, 0:ROWS, :], flips[1])
        others = dot(mirrored[f], flips[0])
        blocks = [first] + [others[ROWS * c : ROWS * (c + 1)] for c in range(SHORT - 1, 0, -1)]
        reverse.append(jnp.concatenate(blocks, axis=0))
    for w, word in enumerate(encode(direct) + encode(reverse)):
        sent[w] = swapped(word)


def make_response(received, flip_rows, flip_lams, response, fields):
    for w in range(4):
        blocks = [
            received[pl.ds((PIECE * v + low) * 6 + 2 + w, ROWS, stride=12), :]
            for low in range(2)
            for v in range(PIECE)
        ]
        word = swap_blocks(jnp.stack(blocks))
        for low in range(2):
            for v in range(PIECE):
                fields[w, pl.ds(LANES * low + v, ROWS, stride=PIECE), :] = word[PIECE * low + v]
    direct = decode(fields[0], fields[1])
    mirror = dot(flip_rows[...], jnp.concatenate(decode(fields[2], fields[3]), axis=1))
    scale = f32(0.5 / (NX * NY))
    top = lax.broadcasted_iota(jnp.int32, (DEVICES, LANES), 0) == 0
    for f in range(4):
        lines = mirror[:, f * LANES : (f + 1) * LANES]
        first = dot(lines[0:ROWS], flip_lams[1])
        lines = dot(lines, flip_lams[0])
        lines = jnp.where(top, jnp.broadcast_to(first[0:1], lines.shape), lines)
        response[f] = (direct[f] + lines if f % 2 == 0 else direct[f] - lines) * scale


def exchange(sent, axis, count):
    width = sent.size // count
    shape = (count, 1, width) if width == 6 * LANES else (count, width // LANES, LANES)
    return lax.all_to_all(
        sent.reshape(shape), axis, split_axis=0, concat_axis=0, tiled=True
    ).reshape(sent.shape)


def on_device(sky_image, observed, noise_weight, basis_tiles, intersection, counts, transfer):
    tables = {name: jnp.asarray(value) for name, value in make_tables().items()}
    band, column = lax.axis_index("sy"), lax.axis_index("sx")
    zero = jnp.zeros((), jnp.int32)
    wanted = lax.dynamic_slice(
        intersection, (2 * band + column // PIECE, zero, zero), (1, SHORT, 4)
    ).reshape(SHORT * 4) - band * LANES

    parts = exchange(
        run(
            pack_inputs,
            shaped(SHORT, TILE_ROWS + 6 * ROWS, LANES, dtype=jnp.bfloat16),
            counts.reshape(2),
            basis_tiles,
            sky_image,
            observed,
            noise_weight,
            scalars=1,
        ),
        "sx",
        SHORT,
    )
    spread = run(
        pack_transfer,
        shaped(4, DEVICES, LANES, dtype=jnp.int32),
        transfer,
        tables["flips"],
        scratch=[pltpu.VMEM((8, DEVICES, LANES), f32)],
    )
    work = [pltpu.VMEM((DEVICES, 2 * LANES), f32)]
    sent, coef, pixels, top, bottom = run(
        first_rows,
        [
            shaped(DEVICES * 6, LANES, dtype=jnp.int32),
            shaped(4, SHORT, ROWS, LANES),
            shaped(SHORT, ROWS, LANES),
            shaped(SHORT, LANES),
            shaped(SHORT, LANES),
        ],
        wanted,
        parts,
        spread,
        tables["turn_x"],
        tables["x_forward"],
        scalars=1,
        scratch=[pltpu.VMEM((SHORT * TILE_ROWS, LANES), f32)] + work,
    )
    received = exchange(sent, EVERY, DEVICES)

    ahead = [(i, (i + 1) % DEVICES) for i in range(DEVICES)]
    behind = [(target, source) for source, target in ahead]
    above = lax.ppermute(bottom, EVERY, ahead)
    below = lax.ppermute(top, EVERY, behind)
    flow = run(variation, shaped(SHORT, ROWS, LANES), pixels, above, below)
    y_tables = [tables[name] for name in ("y_long", "turn_y", "y_forward", "y_inverse")]
    x_tables = [tables[name] for name in ("turn_x", "x_forward", "x_inverse")]
    sent, response = run(
        middle_lines,
        [shaped(DEVICES * 2, LANES), shaped(4, DEVICES, LANES)],
        received,
        tables["flip_rows"],
        tables["flip_lams"],
        *y_tables,
        scratch=[pltpu.VMEM((4, DEVICES, LANES), jnp.int32)],
    )
    received = exchange(sent, EVERY, DEVICES)
    sent, residual = run(
        middle_rows,
        [shaped(DEVICES * 2, LANES), shaped(SHORT, ROWS, LANES)],
        received,
        parts,
        *x_tables,
        scratch=work,
    )
    received = exchange(sent, EVERY, DEVICES)
    sent = run(
        last_lines, shaped(DEVICES * 2, LANES, dtype=jnp.int32), received, response, *y_tables
    )
    received = exchange(sent, EVERY, DEVICES)
    sent = run(
        last_rows,
        shaped(SHORT, 2 * ROWS, LANES),
        received,
        coef,
        residual,
        flow,
        tables["turn_x"],
        tables["x_inverse"],
        scratch=work,
    )
    blocks = exchange(sent, "sx", SHORT)
    gradient = blocks[:, :ROWS, :].reshape(SHORT * ROWS, LANES)
    residual = blocks[:, ROWS:, :].reshape(SHORT * ROWS, LANES)
    return (residual, gradient)


def solution(mesh):
    placed = (
        P("sy", "sx"),
        P("sy", "sx"),
        P("sy", "sx"),
        P(("sy", "sx"), None, None),
        P(),
        P("sy", "sx"),
        P(None, None, ("sy", "sx"), None),
    )
    return jax.shard_map(
        on_device,
        mesh=mesh,
        in_specs=placed,
        out_specs=(P("sy", "sx"), P("sy", "sx")),
        check_vma=False,
    )
```

```python
import math

import jax
import jax.numpy as jnp
import numpy as np
from jax import lax
from jax.experimental import pallas as pl
from jax.experimental.pallas import tpu as pltpu
from jax.sharding import PartitionSpec as P

highest = lax.Precision.HIGHEST
tv_weight = 0.5
smoothing = 0.25
f32 = jnp.float32
SHORT, LANES, ROWS, PIECE = 32, 128, 8, 16
DEVICES = 256
TILE_ROWS = 32
CODE_BITS = 13
NX, NY = 4096, 2048
EVERY = ("sy", "sx")


def table(array):
    return np.asarray(array, np.float32)


def parts_of(array):
    exact = np.asarray(array, np.float32)
    high = exact.astype(jnp.bfloat16)
    return high, (exact - high.astype(np.float32)).astype(jnp.bfloat16)


def on_left(array):
    high, low = parts_of(array)
    return np.concatenate([high, high, low], axis=1)


def on_right(array):
    high, low = parts_of(array)
    return np.concatenate([high, high, low], axis=0)


def circle(left, right, length):
    angles = np.outer(np.arange(left), np.arange(right)) % length * (2.0 * np.pi / length)
    return np.cos(angles), np.sin(angles)


def joined(cos, sin, sign):
    return on_right(np.block([[cos, sign * sin], [-sign * sin, cos]]))


def make_tables():
    cos_turn, sin_turn = circle(SHORT, LANES, NX)
    cos_long, sin_long = circle(LANES, LANES, LANES)
    cos_dev, sin_dev = circle(DEVICES, DEVICES, DEVICES)
    cos_row, sin_row = circle(DEVICES, ROWS, NY)
    cos_eight, sin_eight = circle(ROWS, ROWS, ROWS)
    spread = np.eye(PIECE)
    wide = lambda matrix: np.kron(matrix, spread)
    lane = np.arange(LANES)
    kappa = np.arange(DEVICES)
    flip = np.zeros((LANES, LANES))
    flip[LANES - 1 - lane, lane] = 1.0
    flip_first = np.zeros((LANES, LANES))
    flip_first[(LANES - lane) % LANES, lane] = 1.0
    flip_rows = np.zeros((DEVICES, DEVICES))
    flip_rows[kappa, (DEVICES - kappa) % DEVICES] = 1.0
    lam = np.arange(ROWS)
    flip_lam = np.zeros((ROWS, ROWS))
    flip_lam[ROWS - 1 - lam, lam] = 1.0
    flip_lam_first = np.zeros((ROWS, ROWS))
    flip_lam_first[(ROWS - lam) % ROWS, lam] = 1.0
    return dict(
        turn_x=table(np.stack([cos_turn, sin_turn])),
        x_forward=joined(cos_long, sin_long, -1.0),
        x_inverse=joined(cos_long, sin_long, 1.0),
        y_long=on_left(np.concatenate([cos_dev, sin_dev])),
        turn_y=table(
            np.stack([np.repeat(cos_row, PIECE, axis=1), np.repeat(sin_row, PIECE, axis=1)])
        ),
        y_forward=joined(wide(cos_eight), wide(sin_eight), -1.0),
        y_inverse=joined(wide(cos_eight), wide(sin_eight), 1.0),
        flips=table(np.stack([flip, flip_first])),
        flip_rows=np.tile(flip_rows, (1, 2)).astype(jnp.bfloat16),
        flip_lams=np.stack(
            [np.tile(wide(flip), (2, 1)) for flip in (flip_lam, flip_lam_first)]
        ).astype(jnp.bfloat16),
    )


def dot(left, right):
    return jnp.dot(left, right, precision=highest, preferred_element_type=f32)


def split(value):
    high = value.astype(jnp.bfloat16)
    return high, (value - high.astype(f32)).astype(jnp.bfloat16)


def product(left, right):
    return jnp.dot(left, right, preferred_element_type=f32)


def times_left(factor, value):
    high, low = split(value)
    return product(factor[...], jnp.concatenate([high, low, high], axis=0))


def times_right(value, factor):
    high, low = split(value)
    return product(jnp.concatenate([high, low, high], axis=1), factor[...])


def run(body, shapes, *operands, scalars=0, far=0, scratch=()):
    whole = pl.BlockSpec(memory_space=pltpu.VMEM)
    operands = [
        pltpu.with_memory_space_constraint(operand, pltpu.HBM) if n < far else operand
        for n, operand in enumerate(operands)
    ]
    single = not isinstance(shapes, (list, tuple))
    return pl.pallas_call(
        body,
        out_shape=shapes,
        in_specs=[pl.BlockSpec(memory_space=pltpu.SMEM)] * scalars
        + [pl.BlockSpec(memory_space=pltpu.HBM)] * far
        + [whole] * (len(operands) - scalars - far),
        out_specs=whole if single else [whole] * len(shapes),
        scratch_shapes=list(scratch),
        compiler_params=pltpu.CompilerParams(vmem_limit_bytes=48 * 1024 * 1024),
    )(*operands)


def shaped(*dims, dtype=f32):
    return jax.ShapeDtypeStruct(dims, dtype)


def swap_blocks(field):
    sub = lax.broadcasted_iota(jnp.int32, field.shape, 1)
    group = lax.broadcasted_iota(jnp.int32, field.shape, 2) // PIECE
    for step in (1, 2, 4):
        low = (sub & step) == 0
        shift = PIECE * step
        if step == 4:
            other = pltpu.roll(pltpu.roll(field, shift, 2), step, 1)
        else:
            moved = jnp.where(
                low, pltpu.roll(field, LANES - shift, 2), pltpu.roll(field, shift, 2)
            )
            other = jnp.where(
                low, pltpu.roll(moved, ROWS - step, 1), pltpu.roll(moved, step, 1)
            )
        field = jnp.where(low == ((group & step) == 0), field, other)
    return field


def add(left, right):
    if left is None or right is None:
        return right if left is None else left
    return left + right


def subtract(left, right):
    if right is None:
        return left
    return -right if left is None else left - right


def scaled(value, factor):
    return None if value is None else value * f32(factor)


def turned(real, imag, cos, sin):
    return (
        subtract(scaled(real, cos), scaled(imag, sin)),
        add(scaled(real, sin), scaled(imag, cos)),
    )


def short_transform(points, sign):
    length = len(points)
    if length == 1:
        return points
    even = short_transform(points[0::2], sign)
    odd = short_transform(points[1::2], sign)
    low, high = [], []
    for k in range(length // 2):
        real, imag = odd[k]
        if k == 0:
            part = (real, imag)
        elif 4 * k == length:
            part = (
                (None if imag is None else imag * f32(-sign)),
                (None if real is None else real * f32(sign)),
            )
        else:
            angle = 2.0 * math.pi * k / length
            part = turned(real, imag, math.cos(angle), sign * math.sin(angle))
        low.append((add(even[k][0], part[0]), add(even[k][1], part[1])))
        high.append((subtract(even[k][0], part[0]), subtract(even[k][1], part[1])))
    return low + high


def swapped(field):
    return swap_blocks(field.reshape(SHORT, ROWS, LANES)).reshape(DEVICES, LANES)


def encode(values):
    top = jnp.maximum(
        jnp.maximum(jnp.abs(values[0]), jnp.abs(values[1])),
        jnp.maximum(jnp.abs(values[2]), jnp.abs(values[3])),
    )
    power = jnp.ceil(jnp.log2(jnp.maximum(top, f32(2.0**-100))))
    factor = jnp.exp2(f32(CODE_BITS) - power)
    limit = 2.0**CODE_BITS - 1.0
    codes = [
        jnp.clip(jnp.floor(value * factor + 0.5), -limit, limit).astype(jnp.int32)
        for value in values
    ]
    shared = power.astype(jnp.int32) + 128
    return (
        (codes[0] << 18) | ((codes[1] & 0x3FFF) << 4) | (shared >> 4),
        (codes[2] << 18) | ((codes[3] & 0x3FFF) << 4) | (shared & 15),
    )


def decode(first, second):
    power = (((first & 15) << 4) | (second & 15)) - (128 + CODE_BITS)
    factor = jnp.exp2(power.astype(f32))
    return [
        code.astype(f32) * factor
        for code in (first >> 18, (first << 14) >> 18, second >> 18, (second << 14) >> 18)
    ]


def low_half(field):
    return lax.broadcasted_iota(jnp.int32, field.shape, 1) < field.shape[1] // 2


def paired(field):
    other = pltpu.roll(field, field.shape[1] // 2, 1)
    low = low_half(field)
    return jnp.where(low, field, other), jnp.where(low, other, field)


def encode_pair(real, imag):
    first_real, second_real = paired(real)
    first_imag, second_imag = paired(imag)
    words = encode([first_real, first_imag, second_real, second_imag])
    return jnp.where(low_half(real), *words)


def decode_pair(word):
    values = decode(*paired(word))
    low = low_half(word)
    return jnp.where(low, values[0], values[2]), jnp.where(low, values[1], values[3])


def rows_to_lines(points, turn, matrix, work):
    for c, (real, imag) in enumerate(short_transform(points, -1.0)):
        cos, sin = turn[0, c : c + 1, :], turn[1, c : c + 1, :]
        imag = jnp.zeros_like(real) if imag is None else imag
        work[ROWS * c : ROWS * (c + 1), :LANES] = real * cos + imag * sin
        work[ROWS * c : ROWS * (c + 1), LANES:] = imag * cos - real * sin
    lines = times_right(work[...], matrix)
    return [lines[:, :LANES], lines[:, LANES:]]


def lines_to_rows(real, imag, turn, matrix, work):
    work[...] = times_right(jnp.concatenate([real, imag], axis=1), matrix)
    points = []
    for c in range(SHORT):
        cos, sin = turn[0, c : c + 1, :], turn[1, c : c + 1, :]
        real = work[ROWS * c : ROWS * (c + 1), :LANES]
        imag = work[ROWS * c : ROWS * (c + 1), LANES:]
        points.append((real * cos - imag * sin, real * sin + imag * cos))
    return short_transform(points, 1.0)


def forward_y(received, y_long, turn_y, matrix):
    both = times_left(y_long, jnp.concatenate(received, axis=1))
    by_cos, by_sin = both[:DEVICES], both[DEVICES:]
    cos, sin = turn_y[0], turn_y[1]
    spectra = []
    for f in range(0, len(received), 2):
        at_real = slice(f * LANES, (f + 1) * LANES)
        at_imag = slice((f + 1) * LANES, (f + 2) * LANES)
        real = by_cos[:, at_real] + by_sin[:, at_imag]
        imag = by_cos[:, at_imag] - by_sin[:, at_real]
        lines = jnp.concatenate([real * cos + imag * sin, imag * cos - real * sin], axis=1)
        out = times_right(lines, matrix)
        spectra.append((out[:, :LANES], out[:, LANES:]))
    return spectra


def inverse_y(spectra, y_long, turn_y, matrix):
    cos, sin = turn_y[0], turn_y[1]
    columns = []
    for real, imag in spectra:
        lines = times_right(jnp.concatenate([real, imag], axis=1), matrix)
        real, imag = lines[:, :LANES], lines[:, LANES:]
        columns += [real * cos - imag * sin, real * sin + imag * cos]
    both = times_left(y_long, jnp.concatenate(columns, axis=1))
    by_cos, by_sin = both[:DEVICES], both[DEVICES:]
    fields = []
    for f in range(0, len(columns), 2):
        at_real = slice(f * LANES, (f + 1) * LANES)
        at_imag = slice((f + 1) * LANES, (f + 2) * LANES)
        fields.append(by_cos[:, at_real] - by_sin[:, at_imag])
        fields.append(by_cos[:, at_imag] + by_sin[:, at_real])
    return fields


def every(ref, index, count):
    return ref[pl.ds(index, DEVICES, stride=count), :]


def put(ref, fields, first, count):
    for f, field in enumerate(fields):
        ref[pl.ds(first + f, DEVICES, stride=count), :] = field


def halves(value):
    high = value.astype(jnp.bfloat16).astype(f32)
    return jnp.concatenate([high, value - high], axis=0).astype(jnp.bfloat16)


def pixel(parts, b, field):
    start = TILE_ROWS + 2 * ROWS * field
    both = parts[b, start : start + 2 * ROWS, :].astype(f32)
    return both[:ROWS] + both[ROWS:]


def pack_inputs(*refs):
    sources, sent, held, done = refs[:5], refs[5], refs[6:11], refs[11]
    copies = [
        pltpu.make_async_copy(source, target, done.at[n])
        for n, (source, target) in enumerate(zip(sources, held))
    ]
    for copy in copies:
        copy.start()
    tiles, counts, *fields = held
    copies[0].wait()
    for piece in range(PIECE):
        rows = jnp.concatenate(
            [
                tiles[l, ROWS * piece : ROWS * (piece + 1), :].astype(f32)
                for l in range(tiles.shape[0])
            ],
            axis=0,
        ).astype(jnp.bfloat16)
        sent[piece, :TILE_ROWS, :] = rows
        sent[piece + PIECE, :TILE_ROWS, :] = rows
    copies[1].wait()
    lane = lax.broadcasted_iota(jnp.int32, (ROWS, LANES), 1)
    for f, field in enumerate(fields):
        copies[2 + f].wait()
        start = TILE_ROWS + 2 * ROWS * f
        for r in range(SHORT):
            value = field[ROWS * r : ROWS * (r + 1), :]
            if f == 2:
                value = jnp.where(lane < counts[r // PIECE], -value, value)
            sent[r, start : start + 2 * ROWS, :] = halves(value)


def first_rows(wanted, parts, spread, turn, matrix, sent, coef, pixels, top, bottom, pool, work):
    for h in range(SHORT):
        pool[TILE_ROWS * h : TILE_ROWS * (h + 1), :] = parts[h, :TILE_ROWS, :].astype(f32)
    fields = []
    for p in range(2):
        points = []
        for b in range(SHORT):
            if p == 0:
                sky = pixel(parts, b, 0)
                pixels[b] = sky
                top[b : b + 1, :] = sky[:1]
                bottom[b : b + 1, :] = sky[ROWS - 1 :]
            sky = pixels[b]
            weight = parts[b, TILE_ROWS + 4 * ROWS : TILE_ROWS + 6 * ROWS, :].astype(f32)[:ROWS]
            pair = []
            for k in (2 * p, 2 * p + 1):
                start = pl.multiple_of(wanted[4 * b + k] * ROWS, ROWS)
                mask = jnp.where(weight[:, k : k + 1] < 0.0, f32(1.0), f32(0.0))
                value = pool[pl.ds(start, ROWS), :] * mask
                coef[k, b] = value
                pair.append(value * sky)
            points.append(tuple(pair))
        fields += rows_to_lines(points, turn, matrix, work)
    put(sent, [swapped(word) for word in encode(fields)], 0, 6)
    put(sent, [spread[word] for word in range(4)], 2, 6)


def middle_lines(
    received, flip_rows, flip_lams, y_long, turn_y, forward, inverse, sent, response, fields
):
    make_response(received, flip_rows, flip_lams, response, fields)
    spectra = forward_y(
        decode(every(received, 0, 6), every(received, 1, 6)), y_long, turn_y, forward
    )
    real = imag = 0.0
    for p, (z_real, z_imag) in enumerate(spectra):
        c_real, c_imag = response[2 * p], response[2 * p + 1]
        real = real + z_real * c_real - z_imag * c_imag
        imag = imag + z_real * c_imag + z_imag * c_real
    sent[...] = encode_pair(*inverse_y([(real, imag)], y_long, turn_y, inverse))


def middle_rows(received, parts, turn, forward, inverse, sent, residual, work):
    word = swap_blocks(received[...].reshape(SHORT, ROWS, LANES))
    real, imag = (part.reshape(DEVICES, LANES) for part in decode_pair(word))
    points = lines_to_rows(real, imag, turn, inverse, work)
    values = []
    for b in range(SHORT):
        value = jnp.abs(pixel(parts, b, 2)) * (points[b][0] - pixel(parts, b, 1))
        residual[b] = value
        values.append((value, None))
    fields = rows_to_lines(values, turn, forward, work)
    word = encode_pair(*(field.reshape(SHORT, ROWS, LANES) for field in fields))
    sent[...] = swap_blocks(word).reshape(DEVICES, LANES)


def last_lines(received, response, y_long, turn_y, forward, inverse, sent):
    ((real, imag),) = forward_y(decode_pair(received[...]), y_long, turn_y, forward)
    spectra = []
    for p in range(2):
        c_real, c_imag = response[2 * p], response[2 * p + 1]
        spectra.append((real * c_real + imag * c_imag, imag * c_real - real * c_imag))
    put(sent, encode(inverse_y(spectra, y_long, turn_y, inverse)), 0, 2)


def last_rows(received, coef, residual, flow, turn, inverse, sent, work):
    fields = decode(swapped(every(received, 0, 2)), swapped(every(received, 1, 2)))
    for p in range(2):
        points = lines_to_rows(fields[2 * p], fields[2 * p + 1], turn, inverse, work)
        for b in range(SHORT):
            value = coef[2 * p, b] * points[b][0] + coef[2 * p + 1, b] * points[b][1]
            if p == 0:
                sent[b, 0:ROWS, :] = value + flow[b]
            else:
                sent[b, 0:ROWS, :] += value
    for b in range(SHORT):
        sent[b, ROWS:, :] = residual[b]


def variation(pixels, above, below, flow):
    sky = pixels[...]
    lane = lax.broadcasted_iota(jnp.int32, sky.shape, 2)
    sub = lax.broadcasted_iota(jnp.int32, sky.shape, 1)

    def after(field):
        moved = pltpu.roll(field, LANES - 1, 2)
        following = jnp.concatenate([moved[1:], moved[:1]], axis=0)
        return jnp.where(lane == LANES - 1, following, moved)

    def flows(field, following):
        step_x = after(field) - field
        step_y = following - field
        magnitude = jnp.sqrt(step_x * step_x + step_y * step_y + smoothing)
        return step_x / magnitude, step_y / magnitude

    upper = jnp.broadcast_to(above[...].reshape(SHORT, 1, LANES), sky.shape)
    lower = jnp.broadcast_to(below[...].reshape(SHORT, 1, LANES), sky.shape)
    following = jnp.where(sub == ROWS - 1, lower, pltpu.roll(sky, ROWS - 1, 1))
    flow_x, flow_y = flows(sky, following)
    _, upper_y = flows(upper, sky)
    moved = pltpu.roll(flow_x, 1, 2)
    before_x = jnp.where(
        lane == 0, jnp.concatenate([moved[-1:], moved[:-1]], axis=0), moved
    )
    before_y = jnp.where(sub == 0, upper_y, pltpu.roll(flow_y, 1, 1))
    flow[...] = -tv_weight * (flow_x - before_x + flow_y - before_y)


def pack_transfer(transfer, flips, sent, mirrored):
    for p in range(2):
        for c in range(SHORT):
            at = slice(LANES * c, LANES * (c + 1))
            real_1, imag_1 = transfer[2 * p, 0, :, at], transfer[2 * p, 1, :, at]
            real_2, imag_2 = transfer[2 * p + 1, 0, :, at], transfer[2 * p + 1, 1, :, at]
            rows = slice(ROWS * c, ROWS * (c + 1))
            mirrored[2 * p, rows, :] = real_1 - imag_2
            mirrored[2 * p + 1, rows, :] = imag_1 + real_2
            mirrored[4 + 2 * p, rows, :] = real_1 + imag_2
            mirrored[5 + 2 * p, rows, :] = imag_1 - real_2
    direct, reverse = [], []
    for f in range(4):
        direct.append(mirrored[4 + f])
        first = dot(mirrored[f, 0:ROWS, :], flips[1])
        others = dot(mirrored[f], flips[0])
        blocks = [first] + [others[ROWS * c : ROWS * (c + 1)] for c in range(SHORT - 1, 0, -1)]
        reverse.append(jnp.concatenate(blocks, axis=0))
    for w, word in enumerate(encode(direct) + encode(reverse)):
        sent[w] = swapped(word)


def make_response(received, flip_rows, flip_lams, response, fields):
    for w in range(4):
        blocks = [
            received[pl.ds((PIECE * v + low) * 6 + 2 + w, ROWS, stride=12), :]
            for low in range(2)
            for v in range(PIECE)
        ]
        word = swap_blocks(jnp.stack(blocks))
        for low in range(2):
            for v in range(PIECE):
                fields[w, pl.ds(LANES * low + v, ROWS, stride=PIECE), :] = word[PIECE * low + v]
    direct = decode(fields[0], fields[1])
    high, low = split(jnp.concatenate(decode(fields[2], fields[3]), axis=1))
    mirror = product(flip_rows[...], jnp.concatenate([high, low], axis=0))
    scale = f32(0.5 / (NX * NY))
    top = lax.broadcasted_iota(jnp.int32, (DEVICES, LANES), 0) == 0
    for f in range(4):
        lines = jnp.concatenate(split(mirror[:, f * LANES : (f + 1) * LANES]), axis=1)
        first = product(lines[0 : 2 * ROWS], flip_lams[1])
        lines = product(lines, flip_lams[0])
        lines = jnp.where(top, jnp.broadcast_to(first[0:1], lines.shape), lines)
        response[f] = (direct[f] + lines if f % 2 == 0 else direct[f] - lines) * scale


def exchange(sent, axis, count):
    width = sent.size // count
    shape = (count, 1, width) if width == 6 * LANES else (count, width // LANES, LANES)
    return lax.all_to_all(
        sent.reshape(shape), axis, split_axis=0, concat_axis=0, tiled=True
    ).reshape(sent.shape)


def on_device(sky_image, observed, noise_weight, basis_tiles, intersection, counts, transfer):
    tables = {name: jnp.asarray(value) for name, value in make_tables().items()}
    band, column = lax.axis_index("sy"), lax.axis_index("sx")
    zero = jnp.zeros((), jnp.int32)
    wanted = lax.dynamic_slice(
        intersection, (2 * band + column // PIECE, zero, zero), (1, SHORT, 4)
    ).reshape(SHORT * 4) - band * LANES

    parts = exchange(
        run(
            pack_inputs,
            shaped(SHORT, TILE_ROWS + 6 * ROWS, LANES, dtype=jnp.bfloat16),
            basis_tiles,
            counts.reshape(2),
            sky_image,
            observed,
            noise_weight,
            far=5,
            scratch=[
                pltpu.VMEM(basis_tiles.shape, basis_tiles.dtype),
                pltpu.SMEM((2,), jnp.int32),
            ]
            + [pltpu.VMEM(sky_image.shape, f32)] * 3
            + [pltpu.SemaphoreType.DMA((5,))],
        ),
        "sx",
        SHORT,
    )
    spread = run(
        pack_transfer,
        shaped(4, DEVICES, LANES, dtype=jnp.int32),
        transfer,
        tables["flips"],
        scratch=[pltpu.VMEM((8, DEVICES, LANES), f32)],
    )
    work = [pltpu.VMEM((DEVICES, 2 * LANES), f32)]
    sent, coef, pixels, top, bottom = run(
        first_rows,
        [
            shaped(DEVICES * 6, LANES, dtype=jnp.int32),
            shaped(4, SHORT, ROWS, LANES),
            shaped(SHORT, ROWS, LANES),
            shaped(SHORT, LANES),
            shaped(SHORT, LANES),
        ],
        wanted,
        parts,
        spread,
        tables["turn_x"],
        tables["x_forward"],
        scalars=1,
        scratch=[pltpu.VMEM((SHORT * TILE_ROWS, LANES), f32)] + work,
    )
    received = exchange(sent, EVERY, DEVICES)

    ahead = [(i, (i + 1) % DEVICES) for i in range(DEVICES)]
    behind = [(target, source) for source, target in ahead]
    above = lax.ppermute(bottom, EVERY, ahead)
    below = lax.ppermute(top, EVERY, behind)
    flow = run(variation, shaped(SHORT, ROWS, LANES), pixels, above, below)
    y_tables = [tables[name] for name in ("y_long", "turn_y", "y_forward", "y_inverse")]
    x_tables = [tables[name] for name in ("turn_x", "x_forward", "x_inverse")]
    sent, response = run(
        middle_lines,
        [shaped(DEVICES, LANES, dtype=jnp.int32), shaped(4, DEVICES, LANES)],
        received,
        tables["flip_rows"],
        tables["flip_lams"],
        *y_tables,
        scratch=[pltpu.VMEM((4, DEVICES, LANES), jnp.int32)],
    )
    received = exchange(sent, EVERY, DEVICES)
    sent, residual = run(
        middle_rows,
        [shaped(DEVICES, LANES, dtype=jnp.int32), shaped(SHORT, ROWS, LANES)],
        received,
        parts,
        *x_tables,
        scratch=work,
    )
    received = exchange(sent, EVERY, DEVICES)
    sent = run(
        last_lines, shaped(DEVICES * 2, LANES, dtype=jnp.int32), received, response, *y_tables
    )
    received = exchange(sent, EVERY, DEVICES)
    sent = run(
        last_rows,
        shaped(SHORT, 2 * ROWS, LANES),
        received,
        coef,
        residual,
        flow,
        tables["turn_x"],
        tables["x_inverse"],
        scratch=work,
    )
    blocks = exchange(sent, "sx", SHORT)
    gradient = blocks[:, :ROWS, :].reshape(SHORT * ROWS, LANES)
    residual = blocks[:, ROWS:, :].reshape(SHORT * ROWS, LANES)
    return (residual, gradient)


def solution(mesh):
    placed = (
        P("sy", "sx"),
        P("sy", "sx"),
        P("sy", "sx"),
        P(("sy", "sx"), None, None),
        P(),
        P("sy", "sx"),
        P(None, None, ("sy", "sx"), None),
    )
    return jax.shard_map(
        on_device,
        mesh=mesh,
        in_specs=placed,
        out_specs=(P("sy", "sx"), P("sy", "sx")),
        check_vma=False,
    )
```

```python
import math

import jax
import jax.numpy as jnp
import numpy as np
from jax import lax
from jax.experimental import pallas as pl
from jax.experimental.pallas import tpu as pltpu
from jax.sharding import PartitionSpec as P

tv_weight = 0.5
smoothing = 0.25
f32 = jnp.float32
SHORT, LANES, ROWS, PIECE = 32, 128, 8, 16
DEVICES = 256
TILE_ROWS = 32
CODE_BITS = 13
NX, NY = 4096, 2048
EVERY = ("sy", "sx")


def table(array):
    return np.asarray(array, np.float32)


def parts_of(array):
    exact = np.asarray(array, np.float32)
    high = exact.astype(jnp.bfloat16)
    return high, (exact - high.astype(np.float32)).astype(jnp.bfloat16)


def on_left(array):
    high, low = parts_of(array)
    return np.concatenate([high, high, low], axis=1)


def on_right(array):
    high, low = parts_of(array)
    return np.concatenate([high, high, low], axis=0)


def circle(left, right, length):
    angles = np.outer(np.arange(left), np.arange(right)) % length * (2.0 * np.pi / length)
    return np.cos(angles), np.sin(angles)


def joined(cos, sin, sign):
    return on_right(np.block([[cos, sign * sin], [-sign * sin, cos]]))


def make_tables():
    cos_turn, sin_turn = circle(SHORT, LANES, NX)
    cos_long, sin_long = circle(LANES, LANES, LANES)
    cos_dev, sin_dev = circle(DEVICES, DEVICES, DEVICES)
    cos_row, sin_row = circle(DEVICES, ROWS, NY)
    cos_eight, sin_eight = circle(ROWS, ROWS, ROWS)
    spread = np.eye(PIECE)
    wide = lambda matrix: np.kron(matrix, spread)
    lane = np.arange(LANES)
    flip = np.zeros((LANES, LANES))
    flip[LANES - 1 - lane, lane] = 1.0
    flip_first = np.zeros((LANES, LANES))
    flip_first[(LANES - lane) % LANES, lane] = 1.0
    return dict(
        turn_x=table(np.stack([cos_turn, sin_turn])),
        x_forward=joined(cos_long, sin_long, -1.0),
        x_inverse=joined(cos_long, sin_long, 1.0),
        y_long=on_left(np.concatenate([cos_dev, sin_dev])),
        turn_y=table(
            np.stack([np.repeat(cos_row, PIECE, axis=1), np.repeat(sin_row, PIECE, axis=1)])
        ),
        y_forward=joined(wide(cos_eight), wide(sin_eight), -1.0),
        y_inverse=joined(wide(cos_eight), wide(sin_eight), 1.0),
        flips=np.stack([np.tile(part, (2, 1)) for part in (flip, flip_first)]).astype(
            jnp.bfloat16
        ),
    )


def split(value):
    high = value.astype(jnp.bfloat16)
    return high, (value - high.astype(f32)).astype(jnp.bfloat16)


def product(left, right):
    return jnp.dot(left, right, preferred_element_type=f32)


def times_left(factor, value):
    high, low = split(value)
    return product(factor[...], jnp.concatenate([high, low, high], axis=0))


def times_right(value, factor):
    high, low = split(value)
    return product(jnp.concatenate([high, low, high], axis=1), factor[...])


def run(body, shapes, *operands, scalars=0, far=0, scratch=()):
    whole = pl.BlockSpec(memory_space=pltpu.VMEM)
    outside = pl.BlockSpec(memory_space=pltpu.HBM)
    operands = [
        pltpu.with_memory_space_constraint(operand, pltpu.HBM) if n < far else operand
        for n, operand in enumerate(operands)
    ]
    single = not isinstance(shapes, (list, tuple))
    return pl.pallas_call(
        body,
        out_shape=shapes,
        in_specs=[pl.BlockSpec(memory_space=pltpu.SMEM)] * scalars
        + [outside] * far
        + [whole] * (len(operands) - scalars - far),
        out_specs=outside if far else whole if single else [whole] * len(shapes),
        scratch_shapes=list(scratch),
        compiler_params=pltpu.CompilerParams(vmem_limit_bytes=48 * 1024 * 1024),
    )(*operands)


def shaped(*dims, dtype=f32):
    return jax.ShapeDtypeStruct(dims, dtype)


def swap_blocks(field):
    sub = lax.broadcasted_iota(jnp.int32, field.shape, 1)
    group = lax.broadcasted_iota(jnp.int32, field.shape, 2) // PIECE
    for step in (1, 2, 4):
        low = (sub & step) == 0
        shift = PIECE * step
        if step == 4:
            other = pltpu.roll(pltpu.roll(field, shift, 2), step, 1)
        else:
            moved = jnp.where(
                low, pltpu.roll(field, LANES - shift, 2), pltpu.roll(field, shift, 2)
            )
            other = jnp.where(
                low, pltpu.roll(moved, ROWS - step, 1), pltpu.roll(moved, step, 1)
            )
        field = jnp.where(low == ((group & step) == 0), field, other)
    return field


def add(left, right):
    if left is None or right is None:
        return right if left is None else left
    return left + right


def subtract(left, right):
    if right is None:
        return left
    return -right if left is None else left - right


def scaled(value, factor):
    return None if value is None else value * f32(factor)


def turned(real, imag, cos, sin):
    return (
        subtract(scaled(real, cos), scaled(imag, sin)),
        add(scaled(real, sin), scaled(imag, cos)),
    )


def short_transform(points, sign):
    length = len(points)
    if length == 1:
        return points
    even = short_transform(points[0::2], sign)
    odd = short_transform(points[1::2], sign)
    low, high = [], []
    for k in range(length // 2):
        real, imag = odd[k]
        if k == 0:
            part = (real, imag)
        elif 4 * k == length:
            part = (
                (None if imag is None else imag * f32(-sign)),
                (None if real is None else real * f32(sign)),
            )
        else:
            angle = 2.0 * math.pi * k / length
            part = turned(real, imag, math.cos(angle), sign * math.sin(angle))
        low.append((add(even[k][0], part[0]), add(even[k][1], part[1])))
        high.append((subtract(even[k][0], part[0]), subtract(even[k][1], part[1])))
    return low + high


def swapped(field):
    return swap_blocks(field.reshape(SHORT, ROWS, LANES)).reshape(DEVICES, LANES)


def encode(values):
    top = jnp.maximum(
        jnp.maximum(jnp.abs(values[0]), jnp.abs(values[1])),
        jnp.maximum(jnp.abs(values[2]), jnp.abs(values[3])),
    )
    power = jnp.ceil(jnp.log2(jnp.maximum(top, f32(2.0**-100))))
    factor = jnp.exp2(f32(CODE_BITS) - power)
    limit = 2.0**CODE_BITS - 1.0
    codes = [
        jnp.clip(jnp.floor(value * factor + 0.5), -limit, limit).astype(jnp.int32)
        for value in values
    ]
    shared = power.astype(jnp.int32) + 128
    return (
        (codes[0] << 18) | ((codes[1] & 0x3FFF) << 4) | (shared >> 4),
        (codes[2] << 18) | ((codes[3] & 0x3FFF) << 4) | (shared & 15),
    )


def decode(first, second):
    power = (((first & 15) << 4) | (second & 15)) - (128 + CODE_BITS)
    factor = jnp.exp2(power.astype(f32))
    return [
        code.astype(f32) * factor
        for code in (first >> 18, (first << 14) >> 18, second >> 18, (second << 14) >> 18)
    ]


def low_half(field):
    return lax.broadcasted_iota(jnp.int32, field.shape, 1) < field.shape[1] // 2


def paired(field):
    other = pltpu.roll(field, field.shape[1] // 2, 1)
    low = low_half(field)
    return jnp.where(low, field, other), jnp.where(low, other, field)


def encode_pair(real, imag):
    first_real, second_real = paired(real)
    first_imag, second_imag = paired(imag)
    words = encode([first_real, first_imag, second_real, second_imag])
    return jnp.where(low_half(real), *words)


def decode_pair(word):
    values = decode(*paired(word))
    low = low_half(word)
    return jnp.where(low, values[0], values[2]), jnp.where(low, values[1], values[3])


def rows_to_lines(points, turn, matrix, work):
    for c, (real, imag) in enumerate(short_transform(points, -1.0)):
        cos, sin = turn[0, c : c + 1, :], turn[1, c : c + 1, :]
        imag = jnp.zeros_like(real) if imag is None else imag
        work[ROWS * c : ROWS * (c + 1), :LANES] = real * cos + imag * sin
        work[ROWS * c : ROWS * (c + 1), LANES:] = imag * cos - real * sin
    lines = times_right(work[...], matrix)
    return [lines[:, :LANES], lines[:, LANES:]]


def lines_to_rows(real, imag, turn, matrix, work):
    work[...] = times_right(jnp.concatenate([real, imag], axis=1), matrix)
    points = []
    for c in range(SHORT):
        cos, sin = turn[0, c : c + 1, :], turn[1, c : c + 1, :]
        real = work[ROWS * c : ROWS * (c + 1), :LANES]
        imag = work[ROWS * c : ROWS * (c + 1), LANES:]
        points.append((real * cos - imag * sin, real * sin + imag * cos))
    return short_transform(points, 1.0)


def forward_y(received, y_long, turn_y, matrix):
    both = times_left(y_long, jnp.concatenate(received, axis=1))
    by_cos, by_sin = both[:DEVICES], both[DEVICES:]
    cos, sin = turn_y[0], turn_y[1]
    spectra = []
    for f in range(0, len(received), 2):
        at_real = slice(f * LANES, (f + 1) * LANES)
        at_imag = slice((f + 1) * LANES, (f + 2) * LANES)
        real = by_cos[:, at_real] + by_sin[:, at_imag]
        imag = by_cos[:, at_imag] - by_sin[:, at_real]
        lines = jnp.concatenate([real * cos + imag * sin, imag * cos - real * sin], axis=1)
        out = times_right(lines, matrix)
        spectra.append((out[:, :LANES], out[:, LANES:]))
    return spectra


def inverse_y(spectra, y_long, turn_y, matrix):
    cos, sin = turn_y[0], turn_y[1]
    columns = []
    for real, imag in spectra:
        lines = times_right(jnp.concatenate([real, imag], axis=1), matrix)
        real, imag = lines[:, :LANES], lines[:, LANES:]
        columns += [real * cos - imag * sin, real * sin + imag * cos]
    both = times_left(y_long, jnp.concatenate(columns, axis=1))
    by_cos, by_sin = both[:DEVICES], both[DEVICES:]
    fields = []
    for f in range(0, len(columns), 2):
        at_real = slice(f * LANES, (f + 1) * LANES)
        at_imag = slice((f + 1) * LANES, (f + 2) * LANES)
        fields.append(by_cos[:, at_real] - by_sin[:, at_imag])
        fields.append(by_cos[:, at_imag] + by_sin[:, at_real])
    return fields


def every(ref, index, count):
    return ref[pl.ds(index, DEVICES, stride=count), :]


def put(ref, fields, first, count):
    for f, field in enumerate(fields):
        ref[pl.ds(first + f, DEVICES, stride=count), :] = field


def halves(value):
    high = value.astype(jnp.bfloat16).astype(f32)
    return jnp.concatenate([high, value - high], axis=0).astype(jnp.bfloat16)


def pixel(parts, b, field):
    start = TILE_ROWS + 2 * ROWS * field
    both = parts[b, start : start + 2 * ROWS, :].astype(f32)
    return both[:ROWS] + both[ROWS:]


def pack_inputs(*refs):
    sources, target, held, sent, done, left = refs[:5], refs[5], refs[6:11], *refs[11:]
    copies = [
        pltpu.make_async_copy(source, local, done.at[n])
        for n, (source, local) in enumerate(zip(sources, held))
    ]

    def leave(n, start, stop):
        rows = (slice(None), slice(start, stop), slice(None))
        copy = pltpu.make_async_copy(sent.at[rows], target.at[rows], left.at[n])
        copy.start()
        return copy

    for copy in copies:
        copy.start()
    tiles, counts, *fields = held
    copies[0].wait()
    for piece in range(PIECE):
        rows = jnp.concatenate(
            [
                tiles[l, ROWS * piece : ROWS * (piece + 1), :].astype(f32)
                for l in range(tiles.shape[0])
            ],
            axis=0,
        ).astype(jnp.bfloat16)
        sent[piece, :TILE_ROWS, :] = rows
        sent[piece + PIECE, :TILE_ROWS, :] = rows
    leaving = [leave(0, 0, TILE_ROWS)]
    copies[1].wait()
    lane = lax.broadcasted_iota(jnp.int32, (ROWS, LANES), 1)
    for f, field in enumerate(fields):
        copies[2 + f].wait()
        start = TILE_ROWS + 2 * ROWS * f
        for r in range(SHORT):
            value = field[ROWS * r : ROWS * (r + 1), :]
            if f == 2:
                value = jnp.where(lane < counts[r // PIECE], -value, value)
            sent[r, start : start + 2 * ROWS, :] = halves(value)
        leaving.append(leave(1 + f, start, start + 2 * ROWS))
    for copy in leaving:
        copy.wait()


def first_rows(wanted, parts, spread, turn, matrix, sent, coef, pixels, top, bottom, pool, work):
    for h in range(SHORT):
        pool[TILE_ROWS * h : TILE_ROWS * (h + 1), :] = parts[h, :TILE_ROWS, :].astype(f32)
    fields = []
    for p in range(2):
        points = []
        for b in range(SHORT):
            if p == 0:
                sky = pixel(parts, b, 0)
                pixels[b] = sky
                top[b : b + 1, :] = sky[:1]
                bottom[b : b + 1, :] = sky[ROWS - 1 :]
            sky = pixels[b]
            weight = parts[b, TILE_ROWS + 4 * ROWS : TILE_ROWS + 6 * ROWS, :].astype(f32)[:ROWS]
            pair = []
            for k in (2 * p, 2 * p + 1):
                start = pl.multiple_of(wanted[4 * b + k] * ROWS, ROWS)
                mask = jnp.where(weight[:, k : k + 1] < 0.0, f32(1.0), f32(0.0))
                value = pool[pl.ds(start, ROWS), :] * mask
                coef[k, b] = value
                pair.append(value * sky)
            points.append(tuple(pair))
        fields += rows_to_lines(points, turn, matrix, work)
    put(sent, [swapped(word) for word in encode(fields)], 0, 6)
    put(sent, [spread[word] for word in range(4)], 2, 6)


def middle_lines(received, y_long, turn_y, forward, inverse, sent, response, fields):
    make_response(received, response, fields)
    spectra = forward_y(
        decode(every(received, 0, 6), every(received, 1, 6)), y_long, turn_y, forward
    )
    real = imag = 0.0
    for p, (z_real, z_imag) in enumerate(spectra):
        c_real, c_imag = response[2 * p], response[2 * p + 1]
        real = real + z_real * c_real - z_imag * c_imag
        imag = imag + z_real * c_imag + z_imag * c_real
    sent[...] = encode_pair(*inverse_y([(real, imag)], y_long, turn_y, inverse))


def middle_rows(received, parts, turn, forward, inverse, sent, residual, work):
    word = swap_blocks(received[...].reshape(SHORT, ROWS, LANES))
    real, imag = (part.reshape(DEVICES, LANES) for part in decode_pair(word))
    points = lines_to_rows(real, imag, turn, inverse, work)
    values = []
    for b in range(SHORT):
        value = jnp.abs(pixel(parts, b, 2)) * (points[b][0] - pixel(parts, b, 1))
        residual[b] = value
        values.append((value, None))
    fields = rows_to_lines(values, turn, forward, work)
    word = encode_pair(*(field.reshape(SHORT, ROWS, LANES) for field in fields))
    sent[...] = swap_blocks(word).reshape(DEVICES, LANES)


def last_lines(received, response, y_long, turn_y, forward, inverse, sent):
    ((real, imag),) = forward_y(decode_pair(received[...]), y_long, turn_y, forward)
    spectra = []
    for p in range(2):
        c_real, c_imag = response[2 * p], response[2 * p + 1]
        spectra.append((real * c_real + imag * c_imag, imag * c_real - real * c_imag))
    put(sent, encode(inverse_y(spectra, y_long, turn_y, inverse)), 0, 2)


def last_rows(received, coef, residual, flow, turn, inverse, sent, work):
    fields = decode(swapped(every(received, 0, 2)), swapped(every(received, 1, 2)))
    for p in range(2):
        points = lines_to_rows(fields[2 * p], fields[2 * p + 1], turn, inverse, work)
        for b in range(SHORT):
            value = coef[2 * p, b] * points[b][0] + coef[2 * p + 1, b] * points[b][1]
            if p == 0:
                sent[b, 0:ROWS, :] = value + flow[b]
            else:
                sent[b, 0:ROWS, :] += value
    for b in range(SHORT):
        sent[b, ROWS:, :] = residual[b]


def variation(pixels, above, below, flow):
    sky = pixels[...]
    lane = lax.broadcasted_iota(jnp.int32, sky.shape, 2)
    sub = lax.broadcasted_iota(jnp.int32, sky.shape, 1)

    def after(field):
        moved = pltpu.roll(field, LANES - 1, 2)
        following = jnp.concatenate([moved[1:], moved[:1]], axis=0)
        return jnp.where(lane == LANES - 1, following, moved)

    def flows(field, following):
        step_x = after(field) - field
        step_y = following - field
        magnitude = jnp.sqrt(step_x * step_x + step_y * step_y + smoothing)
        return step_x / magnitude, step_y / magnitude

    upper = jnp.broadcast_to(above[...].reshape(SHORT, 1, LANES), sky.shape)
    lower = jnp.broadcast_to(below[...].reshape(SHORT, 1, LANES), sky.shape)
    following = jnp.where(sub == ROWS - 1, lower, pltpu.roll(sky, ROWS - 1, 1))
    flow_x, flow_y = flows(sky, following)
    _, upper_y = flows(upper, sky)
    moved = pltpu.roll(flow_x, 1, 2)
    before_x = jnp.where(
        lane == 0, jnp.concatenate([moved[-1:], moved[:-1]], axis=0), moved
    )
    before_y = jnp.where(sub == 0, upper_y, pltpu.roll(flow_y, 1, 1))
    flow[...] = -tv_weight * (flow_x - before_x + flow_y - before_y)


def reversed_rows(field):
    sub = lax.broadcasted_iota(jnp.int32, field.shape, 1)
    for step in (1, 2):
        field = jnp.where(
            (sub & step) == 0, pltpu.roll(field, ROWS - step, 1), pltpu.roll(field, step, 1)
        )
    return pltpu.roll(field, 4, 1)


def pack_transfer(special, transfer, flips, sent, mirrored):
    for p in range(2):
        for c in range(SHORT):
            at = slice(LANES * c, LANES * (c + 1))
            real_1, imag_1 = transfer[2 * p, 0, :, at], transfer[2 * p, 1, :, at]
            real_2, imag_2 = transfer[2 * p + 1, 0, :, at], transfer[2 * p + 1, 1, :, at]
            rows = slice(ROWS * c, ROWS * (c + 1))
            mirrored[2 * p, rows, :] = real_1 - imag_2
            mirrored[2 * p + 1, rows, :] = imag_1 + real_2
            mirrored[4 + 2 * p, rows, :] = real_1 + imag_2
            mirrored[5 + 2 * p, rows, :] = imag_1 - real_2
    direct, reverse = [], []
    for f in range(4):
        direct.append(mirrored[4 + f])
        first = product(jnp.concatenate(split(mirrored[f, 0 : 2 * ROWS, :]), axis=1), flips[1])
        others = product(jnp.concatenate(split(mirrored[f]), axis=1), flips[0])
        blocks = [first[:ROWS]]
        blocks += [others[ROWS * c : ROWS * (c + 1)] for c in range(SHORT - 1, 0, -1)]
        reverse.append(jnp.concatenate(blocks, axis=0))
    for w, word in enumerate(encode(direct)):
        sent[w] = swapped(word)
    for w, word in enumerate(encode(reverse)):
        word = reversed_rows(word.reshape(SHORT, ROWS, LANES))
        word = jnp.where(special[0] == 1, pltpu.roll(word, 1, 1), word)
        sent[2 + w] = swap_blocks(word).reshape(DEVICES, LANES)


def mirrored_blocks(blocks):
    flipped = reversed_rows(jnp.stack(blocks))
    of = lambda low, v: flipped[PIECE * low + v : PIECE * low + v + 1]
    head = lax.broadcasted_iota(jnp.int32, (1, ROWS, LANES), 2) < PIECE
    ordered = []
    for low in range(2):
        own = pltpu.roll(of(0, 0), 1, 1) if low == 0 else of(1, 0)
        ordered.append(jnp.where(head, own, of(1 - low, 0)))
        ordered += [of(1 - low, PIECE - v) for v in range(1, PIECE)]
    return jnp.concatenate(ordered, axis=0)


def make_response(received, response, fields):
    for w in range(4):
        blocks = [
            received[pl.ds((PIECE * v + low) * 6 + 2 + w, ROWS, stride=12), :]
            for low in range(2)
            for v in range(PIECE)
        ]
        word = swap_blocks(jnp.stack(blocks) if w < 2 else mirrored_blocks(blocks))
        for low in range(2):
            for v in range(PIECE):
                fields[w, pl.ds(LANES * low + v, ROWS, stride=PIECE), :] = word[PIECE * low + v]
    scale = f32(0.5 / (NX * NY))
    direct, mirror = decode(fields[0], fields[1]), decode(fields[2], fields[3])
    for f in range(4):
        response[f] = (direct[f] + mirror[f] if f % 2 == 0 else direct[f] - mirror[f]) * scale


def exchange(sent, axis, count):
    width = sent.size // count
    shape = (count, 1, width) if width == 6 * LANES else (count, width // LANES, LANES)
    return lax.all_to_all(
        sent.reshape(shape), axis, split_axis=0, concat_axis=0, tiled=True
    ).reshape(sent.shape)


def on_device(sky_image, observed, noise_weight, basis_tiles, intersection, counts, transfer):
    tables = {name: jnp.asarray(value) for name, value in make_tables().items()}
    band, column = lax.axis_index("sy"), lax.axis_index("sx")
    zero = jnp.zeros((), jnp.int32)
    wanted = lax.dynamic_slice(
        intersection, (2 * band + column // PIECE, zero, zero), (1, SHORT, 4)
    ).reshape(SHORT * 4) - band * LANES

    parts = exchange(
        run(
            pack_inputs,
            shaped(SHORT, TILE_ROWS + 6 * ROWS, LANES, dtype=jnp.bfloat16),
            basis_tiles,
            counts.reshape(2),
            sky_image,
            observed,
            noise_weight,
            far=5,
            scratch=[
                pltpu.VMEM(basis_tiles.shape, basis_tiles.dtype),
                pltpu.SMEM((2,), jnp.int32),
            ]
            + [pltpu.VMEM(sky_image.shape, f32)] * 3
            + [
                pltpu.VMEM((SHORT, TILE_ROWS + 6 * ROWS, LANES), jnp.bfloat16),
                pltpu.SemaphoreType.DMA((5,)),
                pltpu.SemaphoreType.DMA((4,)),
            ],
        ),
        "sx",
        SHORT,
    )
    special = jnp.where(band * SHORT + column < PIECE, 1, 0).astype(jnp.int32).reshape(1)
    spread = run(
        pack_transfer,
        shaped(4, DEVICES, LANES, dtype=jnp.int32),
        special,
        transfer,
        tables["flips"],
        scalars=1,
        scratch=[pltpu.VMEM((8, DEVICES, LANES), f32)],
    )
    work = [pltpu.VMEM((DEVICES, 2 * LANES), f32)]
    sent, coef, pixels, top, bottom = run(
        first_rows,
        [
            shaped(DEVICES * 6, LANES, dtype=jnp.int32),
            shaped(4, SHORT, ROWS, LANES),
            shaped(SHORT, ROWS, LANES),
            shaped(SHORT, LANES),
            shaped(SHORT, LANES),
        ],
        wanted,
        parts,
        spread,
        tables["turn_x"],
        tables["x_forward"],
        scalars=1,
        scratch=[pltpu.VMEM((SHORT * TILE_ROWS, LANES), f32)] + work,
    )
    received = exchange(sent, EVERY, DEVICES)

    ahead = [(i, (i + 1) % DEVICES) for i in range(DEVICES)]
    behind = [(target, source) for source, target in ahead]
    above = lax.ppermute(bottom, EVERY, ahead)
    below = lax.ppermute(top, EVERY, behind)
    flow = run(variation, shaped(SHORT, ROWS, LANES), pixels, above, below)
    y_tables = [tables[name] for name in ("y_long", "turn_y", "y_forward", "y_inverse")]
    x_tables = [tables[name] for name in ("turn_x", "x_forward", "x_inverse")]
    sent, response = run(
        middle_lines,
        [shaped(DEVICES, LANES, dtype=jnp.int32), shaped(4, DEVICES, LANES)],
        received,
        *y_tables,
        scratch=[pltpu.VMEM((4, DEVICES, LANES), jnp.int32)],
    )
    received = exchange(sent, EVERY, DEVICES)
    sent, residual = run(
        middle_rows,
        [shaped(DEVICES, LANES, dtype=jnp.int32), shaped(SHORT, ROWS, LANES)],
        received,
        parts,
        *x_tables,
        scratch=work,
    )
    received = exchange(sent, EVERY, DEVICES)
    sent = run(
        last_lines, shaped(DEVICES * 2, LANES, dtype=jnp.int32), received, response, *y_tables
    )
    received = exchange(sent, EVERY, DEVICES)
    sent = run(
        last_rows,
        shaped(SHORT, 2 * ROWS, LANES),
        received,
        coef,
        residual,
        flow,
        tables["turn_x"],
        tables["x_inverse"],
        scratch=work,
    )
    blocks = exchange(sent, "sx", SHORT)
    gradient = blocks[:, :ROWS, :].reshape(SHORT * ROWS, LANES)
    residual = blocks[:, ROWS:, :].reshape(SHORT * ROWS, LANES)
    return (residual, gradient)


def solution(mesh):
    placed = (
        P("sy", "sx"),
        P("sy", "sx"),
        P("sy", "sx"),
        P(("sy", "sx"), None, None),
        P(),
        P("sy", "sx"),
        P(None, None, ("sy", "sx"), None),
    )
    return jax.shard_map(
        on_device,
        mesh=mesh,
        in_specs=placed,
        out_specs=(P("sy", "sx"), P("sy", "sx")),
        check_vma=False,
    )
```

```python
import math

import jax
import jax.numpy as jnp
import numpy as np
from jax import lax
from jax.experimental import pallas as pl
from jax.experimental.pallas import tpu as pltpu
from jax.sharding import PartitionSpec as P

tv_weight = 0.5
smoothing = 0.25
f32 = jnp.float32
SHORT, LANES, ROWS, PIECE = 32, 128, 8, 16
DEVICES = 256
TILE_ROWS = 32
CODE_BITS = 13
NX, NY = 4096, 2048
EVERY = ("sy", "sx")


def table(array):
    return np.asarray(array, np.float32)


def parts_of(array):
    exact = np.asarray(array, np.float32)
    high = exact.astype(jnp.bfloat16)
    return high, (exact - high.astype(np.float32)).astype(jnp.bfloat16)


def on_left(array):
    high, low = parts_of(array)
    return np.concatenate([high, high, low], axis=1)


def on_right(array):
    high, low = parts_of(array)
    return np.concatenate([high, high, low], axis=0)


def circle(left, right, length):
    angles = np.outer(np.arange(left), np.arange(right)) % length * (2.0 * np.pi / length)
    return np.cos(angles), np.sin(angles)


def joined(cos, sin, sign):
    return on_right(np.block([[cos, sign * sin], [-sign * sin, cos]]))


def make_tables():
    cos_turn, sin_turn = circle(SHORT, LANES, NX)
    cos_long, sin_long = circle(LANES, LANES, LANES)
    cos_dev, sin_dev = circle(DEVICES, DEVICES, DEVICES)
    cos_row, sin_row = circle(DEVICES, ROWS, NY)
    cos_eight, sin_eight = circle(ROWS, ROWS, ROWS)
    spread = np.eye(PIECE)
    wide = lambda matrix: np.kron(matrix, spread)
    lane = np.arange(LANES)
    flip = np.zeros((LANES, LANES))
    flip[LANES - 1 - lane, lane] = 1.0
    flip_first = np.zeros((LANES, LANES))
    flip_first[(LANES - lane) % LANES, lane] = 1.0
    return dict(
        turn_x=table(np.stack([cos_turn, sin_turn])),
        x_forward=joined(cos_long, sin_long, -1.0),
        x_inverse=joined(cos_long, sin_long, 1.0),
        y_long=on_left(np.concatenate([cos_dev, sin_dev])),
        turn_y=table(
            np.stack([np.repeat(cos_row, PIECE, axis=1), np.repeat(sin_row, PIECE, axis=1)])
        ),
        y_forward=joined(wide(cos_eight), wide(sin_eight), -1.0),
        y_inverse=joined(wide(cos_eight), wide(sin_eight), 1.0),
        flips=np.stack([np.tile(part, (2, 1)) for part in (flip, flip_first)]).astype(
            jnp.bfloat16
        ),
    )


def split(value):
    high = value.astype(jnp.bfloat16)
    return high, (value - high.astype(f32)).astype(jnp.bfloat16)


def product(left, right):
    return jnp.dot(left, right, preferred_element_type=f32)


def times_left(factor, value):
    high, low = split(value)
    return product(factor[...], jnp.concatenate([high, low, high], axis=0))


def times_right(value, factor):
    high, low = split(value)
    return product(jnp.concatenate([high, low, high], axis=1), factor[...])


def run(body, shapes, *operands, scalars=0, far=0, scratch=()):
    whole = pl.BlockSpec(memory_space=pltpu.VMEM)
    outside = pl.BlockSpec(memory_space=pltpu.HBM)
    operands = [
        pltpu.with_memory_space_constraint(operand, pltpu.HBM) if n < far else operand
        for n, operand in enumerate(operands)
    ]
    single = not isinstance(shapes, (list, tuple))
    return pl.pallas_call(
        body,
        out_shape=shapes,
        in_specs=[pl.BlockSpec(memory_space=pltpu.SMEM)] * scalars
        + [outside] * far
        + [whole] * (len(operands) - scalars - far),
        out_specs=outside if far else whole if single else [whole] * len(shapes),
        scratch_shapes=list(scratch),
        compiler_params=pltpu.CompilerParams(vmem_limit_bytes=48 * 1024 * 1024),
    )(*operands)


def shaped(*dims, dtype=f32):
    return jax.ShapeDtypeStruct(dims, dtype)


def swap_blocks(field):
    sub = lax.broadcasted_iota(jnp.int32, field.shape, 1)
    group = lax.broadcasted_iota(jnp.int32, field.shape, 2) // PIECE
    for step in (1, 2, 4):
        low = (sub & step) == 0
        shift = PIECE * step
        if step == 4:
            other = pltpu.roll(pltpu.roll(field, shift, 2), step, 1)
        else:
            moved = jnp.where(
                low, pltpu.roll(field, LANES - shift, 2), pltpu.roll(field, shift, 2)
            )
            other = jnp.where(
                low, pltpu.roll(moved, ROWS - step, 1), pltpu.roll(moved, step, 1)
            )
        field = jnp.where(low == ((group & step) == 0), field, other)
    return field


def add(left, right):
    if left is None or right is None:
        return right if left is None else left
    return left + right


def subtract(left, right):
    if right is None:
        return left
    return -right if left is None else left - right


def scaled(value, factor):
    return None if value is None else value * f32(factor)


def turned(real, imag, cos, sin):
    return (
        subtract(scaled(real, cos), scaled(imag, sin)),
        add(scaled(real, sin), scaled(imag, cos)),
    )


def short_transform(points, sign):
    length = len(points)
    if length == 1:
        return points
    even = short_transform(points[0::2], sign)
    odd = short_transform(points[1::2], sign)
    low, high = [], []
    for k in range(length // 2):
        real, imag = odd[k]
        if k == 0:
            part = (real, imag)
        elif 4 * k == length:
            part = (
                (None if imag is None else imag * f32(-sign)),
                (None if real is None else real * f32(sign)),
            )
        else:
            angle = 2.0 * math.pi * k / length
            part = turned(real, imag, math.cos(angle), sign * math.sin(angle))
        low.append((add(even[k][0], part[0]), add(even[k][1], part[1])))
        high.append((subtract(even[k][0], part[0]), subtract(even[k][1], part[1])))
    return low + high


def swapped(field):
    return swap_blocks(field.reshape(SHORT, ROWS, LANES)).reshape(DEVICES, LANES)


def encode(values):
    top = jnp.maximum(
        jnp.maximum(jnp.abs(values[0]), jnp.abs(values[1])),
        jnp.maximum(jnp.abs(values[2]), jnp.abs(values[3])),
    )
    power = jnp.ceil(jnp.log2(jnp.maximum(top, f32(2.0**-100))))
    factor = jnp.exp2(f32(CODE_BITS) - power)
    limit = 2.0**CODE_BITS - 1.0
    codes = [
        jnp.clip(jnp.floor(value * factor + 0.5), -limit, limit).astype(jnp.int32)
        for value in values
    ]
    shared = power.astype(jnp.int32) + 128
    return (
        (codes[0] << 18) | ((codes[1] & 0x3FFF) << 4) | (shared >> 4),
        (codes[2] << 18) | ((codes[3] & 0x3FFF) << 4) | (shared & 15),
    )


def decode(first, second):
    power = (((first & 15) << 4) | (second & 15)) - (128 + CODE_BITS)
    factor = jnp.exp2(power.astype(f32))
    return [
        code.astype(f32) * factor
        for code in (first >> 18, (first << 14) >> 18, second >> 18, (second << 14) >> 18)
    ]


def low_half(field):
    return lax.broadcasted_iota(jnp.int32, field.shape, 1) < field.shape[1] // 2


def paired(field):
    other = pltpu.roll(field, field.shape[1] // 2, 1)
    low = low_half(field)
    return jnp.where(low, field, other), jnp.where(low, other, field)


def encode_pair(real, imag):
    first_real, second_real = paired(real)
    first_imag, second_imag = paired(imag)
    words = encode([first_real, first_imag, second_real, second_imag])
    return jnp.where(low_half(real), *words)


def decode_pair(word):
    values = decode(*paired(word))
    low = low_half(word)
    return jnp.where(low, values[0], values[2]), jnp.where(low, values[1], values[3])


def rows_to_lines(points, turn, matrix, work):
    for c, (real, imag) in enumerate(short_transform(points, -1.0)):
        cos, sin = turn[0, c : c + 1, :], turn[1, c : c + 1, :]
        imag = jnp.zeros_like(real) if imag is None else imag
        work[ROWS * c : ROWS * (c + 1), :LANES] = real * cos + imag * sin
        work[ROWS * c : ROWS * (c + 1), LANES:] = imag * cos - real * sin
    lines = times_right(work[...], matrix)
    return [lines[:, :LANES], lines[:, LANES:]]


def lines_to_rows(real, imag, turn, matrix, work):
    work[...] = times_right(jnp.concatenate([real, imag], axis=1), matrix)
    points = []
    for c in range(SHORT):
        cos, sin = turn[0, c : c + 1, :], turn[1, c : c + 1, :]
        real = work[ROWS * c : ROWS * (c + 1), :LANES]
        imag = work[ROWS * c : ROWS * (c + 1), LANES:]
        points.append((real * cos - imag * sin, real * sin + imag * cos))
    return short_transform(points, 1.0)


def forward_y(received, y_long, turn_y, matrix):
    both = times_left(y_long, jnp.concatenate(received, axis=1))
    by_cos, by_sin = both[:DEVICES], both[DEVICES:]
    cos, sin = turn_y[0], turn_y[1]
    spectra = []
    for f in range(0, len(received), 2):
        at_real = slice(f * LANES, (f + 1) * LANES)
        at_imag = slice((f + 1) * LANES, (f + 2) * LANES)
        real = by_cos[:, at_real] + by_sin[:, at_imag]
        imag = by_cos[:, at_imag] - by_sin[:, at_real]
        lines = jnp.concatenate([real * cos + imag * sin, imag * cos - real * sin], axis=1)
        out = times_right(lines, matrix)
        spectra.append((out[:, :LANES], out[:, LANES:]))
    return spectra


def inverse_y(spectra, y_long, turn_y, matrix):
    cos, sin = turn_y[0], turn_y[1]
    columns = []
    for real, imag in spectra:
        lines = times_right(jnp.concatenate([real, imag], axis=1), matrix)
        real, imag = lines[:, :LANES], lines[:, LANES:]
        columns += [real * cos - imag * sin, real * sin + imag * cos]
    both = times_left(y_long, jnp.concatenate(columns, axis=1))
    by_cos, by_sin = both[:DEVICES], both[DEVICES:]
    fields = []
    for f in range(0, len(columns), 2):
        at_real = slice(f * LANES, (f + 1) * LANES)
        at_imag = slice((f + 1) * LANES, (f + 2) * LANES)
        fields.append(by_cos[:, at_real] - by_sin[:, at_imag])
        fields.append(by_cos[:, at_imag] + by_sin[:, at_real])
    return fields


def every(ref, index, count):
    return ref[pl.ds(index, DEVICES, stride=count), :]


def put(ref, fields, first, count):
    for f, field in enumerate(fields):
        ref[pl.ds(first + f, DEVICES, stride=count), :] = field


def halves(value):
    high = value.astype(jnp.bfloat16).astype(f32)
    return jnp.concatenate([high, value - high], axis=0).astype(jnp.bfloat16)


def pixel(parts, b, field):
    start = TILE_ROWS + 2 * ROWS * field
    both = parts[b, start : start + 2 * ROWS, :].astype(f32)
    return both[:ROWS] + both[ROWS:]


def pack_inputs(*refs):
    sources, target, held, sent, done, left = refs[:5], refs[5], refs[6:11], *refs[11:]
    copies = [
        pltpu.make_async_copy(source, local, done.at[n])
        for n, (source, local) in enumerate(zip(sources, held))
    ]

    def leave(n, start, stop):
        rows = (slice(None), slice(start, stop), slice(None))
        copy = pltpu.make_async_copy(sent.at[rows], target.at[rows], left.at[n])
        copy.start()
        return copy

    for copy in copies:
        copy.start()
    tiles, counts, *fields = held
    copies[0].wait()
    for piece in range(PIECE):
        rows = jnp.concatenate(
            [
                tiles[l, ROWS * piece : ROWS * (piece + 1), :].astype(f32)
                for l in range(tiles.shape[0])
            ],
            axis=0,
        ).astype(jnp.bfloat16)
        sent[piece, :TILE_ROWS, :] = rows
        sent[piece + PIECE, :TILE_ROWS, :] = rows
    leaving = [leave(0, 0, TILE_ROWS)]
    copies[1].wait()
    lane = lax.broadcasted_iota(jnp.int32, (ROWS, LANES), 1)
    for f, field in enumerate(fields):
        copies[2 + f].wait()
        start = TILE_ROWS + 2 * ROWS * f
        for r in range(SHORT):
            value = field[ROWS * r : ROWS * (r + 1), :]
            if f == 2:
                value = jnp.where(lane < counts[r // PIECE], -value, value)
            sent[r, start : start + 2 * ROWS, :] = halves(value)
        leaving.append(leave(1 + f, start, start + 2 * ROWS))
    for copy in leaving:
        copy.wait()


def first_rows(wanted, parts, spread, turn, matrix, sent, coef, pixels, top, bottom, pool, work):
    for h in range(SHORT):
        pool[TILE_ROWS * h : TILE_ROWS * (h + 1), :] = parts[h, :TILE_ROWS, :].astype(f32)
    fields = []
    for p in range(2):
        points = []
        for b in range(SHORT):
            if p == 0:
                sky = pixel(parts, b, 0)
                pixels[b] = sky
                top[b : b + 1, :] = sky[:1]
                bottom[b : b + 1, :] = sky[ROWS - 1 :]
            sky = pixels[b]
            weight = parts[b, TILE_ROWS + 4 * ROWS : TILE_ROWS + 6 * ROWS, :].astype(f32)[:ROWS]
            pair = []
            for k in (2 * p, 2 * p + 1):
                start = pl.multiple_of(wanted[4 * b + k] * ROWS, ROWS)
                mask = jnp.where(weight[:, k : k + 1] < 0.0, f32(1.0), f32(0.0))
                value = pool[pl.ds(start, ROWS), :] * mask
                coef[k, b] = value
                pair.append(value * sky)
            points.append(tuple(pair))
        fields += rows_to_lines(points, turn, matrix, work)
    sent[...] = spread[...]
    put(sent, [swapped(word) for word in encode(fields)], 0, 6)


def middle_lines(received, y_long, turn_y, forward, inverse, sent, response, fields):
    make_response(received, response, fields)
    spectra = forward_y(
        decode(every(received, 0, 6), every(received, 1, 6)), y_long, turn_y, forward
    )
    real = imag = 0.0
    for p, (z_real, z_imag) in enumerate(spectra):
        c_real, c_imag = response[2 * p], response[2 * p + 1]
        real = real + z_real * c_real - z_imag * c_imag
        imag = imag + z_real * c_imag + z_imag * c_real
    sent[...] = encode_pair(*inverse_y([(real, imag)], y_long, turn_y, inverse))


def middle_rows(received, parts, turn, forward, inverse, sent, residual, work):
    word = swap_blocks(received[...].reshape(SHORT, ROWS, LANES))
    real, imag = (part.reshape(DEVICES, LANES) for part in decode_pair(word))
    points = lines_to_rows(real, imag, turn, inverse, work)
    values = []
    for b in range(SHORT):
        value = jnp.abs(pixel(parts, b, 2)) * (points[b][0] - pixel(parts, b, 1))
        residual[b] = value
        values.append((value, None))
    fields = rows_to_lines(values, turn, forward, work)
    word = encode_pair(*(field.reshape(SHORT, ROWS, LANES) for field in fields))
    sent[...] = swap_blocks(word).reshape(DEVICES, LANES)


def last_lines(received, response, y_long, turn_y, forward, inverse, sent):
    ((real, imag),) = forward_y(decode_pair(received[...]), y_long, turn_y, forward)
    spectra = []
    for p in range(2):
        c_real, c_imag = response[2 * p], response[2 * p + 1]
        spectra.append((real * c_real + imag * c_imag, imag * c_real - real * c_imag))
    put(sent, encode(inverse_y(spectra, y_long, turn_y, inverse)), 0, 2)


def last_rows(received, coef, residual, flow, turn, inverse, sent, work):
    fields = decode(swapped(every(received, 0, 2)), swapped(every(received, 1, 2)))
    for p in range(2):
        points = lines_to_rows(fields[2 * p], fields[2 * p + 1], turn, inverse, work)
        for b in range(SHORT):
            value = coef[2 * p, b] * points[b][0] + coef[2 * p + 1, b] * points[b][1]
            if p == 0:
                sent[b, 0:ROWS, :] = value + flow[b]
            else:
                sent[b, 0:ROWS, :] += value
    for b in range(SHORT):
        sent[b, ROWS:, :] = residual[b]


def variation(pixels, above, below, flow):
    sky = pixels[...]
    lane = lax.broadcasted_iota(jnp.int32, sky.shape, 2)
    sub = lax.broadcasted_iota(jnp.int32, sky.shape, 1)

    def after(field):
        moved = pltpu.roll(field, LANES - 1, 2)
        following = jnp.concatenate([moved[1:], moved[:1]], axis=0)
        return jnp.where(lane == LANES - 1, following, moved)

    def flows(field, following):
        step_x = after(field) - field
        step_y = following - field
        magnitude = jnp.sqrt(step_x * step_x + step_y * step_y + smoothing)
        return step_x / magnitude, step_y / magnitude

    upper = jnp.broadcast_to(above[...].reshape(SHORT, 1, LANES), sky.shape)
    lower = jnp.broadcast_to(below[...].reshape(SHORT, 1, LANES), sky.shape)
    following = jnp.where(sub == ROWS - 1, lower, pltpu.roll(sky, ROWS - 1, 1))
    flow_x, flow_y = flows(sky, following)
    _, upper_y = flows(upper, sky)
    moved = pltpu.roll(flow_x, 1, 2)
    before_x = jnp.where(
        lane == 0, jnp.concatenate([moved[-1:], moved[:-1]], axis=0), moved
    )
    before_y = jnp.where(sub == 0, upper_y, pltpu.roll(flow_y, 1, 1))
    flow[...] = -tv_weight * (flow_x - before_x + flow_y - before_y)


def reversed_rows(field):
    sub = lax.broadcasted_iota(jnp.int32, field.shape, 1)
    for step in (1, 2):
        field = jnp.where(
            (sub & step) == 0, pltpu.roll(field, ROWS - step, 1), pltpu.roll(field, step, 1)
        )
    return pltpu.roll(field, 4, 1)


def pack_transfer(special, transfer, flips, sent, mirrored):
    for p in range(2):
        for c in range(SHORT):
            at = slice(LANES * c, LANES * (c + 1))
            real_1, imag_1 = transfer[2 * p, 0, :, at], transfer[2 * p, 1, :, at]
            real_2, imag_2 = transfer[2 * p + 1, 0, :, at], transfer[2 * p + 1, 1, :, at]
            rows = slice(ROWS * c, ROWS * (c + 1))
            mirrored[2 * p, rows, :] = real_1 - imag_2
            mirrored[2 * p + 1, rows, :] = imag_1 + real_2
            mirrored[4 + 2 * p, rows, :] = real_1 + imag_2
            mirrored[5 + 2 * p, rows, :] = imag_1 - real_2
    direct, reverse = [], []
    for f in range(4):
        direct.append(mirrored[4 + f])
        first = product(jnp.concatenate(split(mirrored[f, 0 : 2 * ROWS, :]), axis=1), flips[1])
        others = product(jnp.concatenate(split(mirrored[f]), axis=1), flips[0])
        blocks = [first[:ROWS]]
        blocks += [others[ROWS * c : ROWS * (c + 1)] for c in range(SHORT - 1, 0, -1)]
        reverse.append(jnp.concatenate(blocks, axis=0))
    put(sent, [jnp.zeros((DEVICES, LANES), jnp.int32)] * 2, 0, 6)
    put(sent, [swapped(word) for word in encode(direct)], 2, 6)
    for w, word in enumerate(encode(reverse)):
        word = reversed_rows(word.reshape(SHORT, ROWS, LANES))
        word = jnp.where(special[0] == 1, pltpu.roll(word, 1, 1), word)
        put(sent, [swap_blocks(word).reshape(DEVICES, LANES)], 4 + w, 6)


def mirrored_blocks(blocks):
    flipped = reversed_rows(jnp.stack(blocks))
    of = lambda low, v: flipped[PIECE * low + v : PIECE * low + v + 1]
    head = lax.broadcasted_iota(jnp.int32, (1, ROWS, LANES), 2) < PIECE
    ordered = []
    for low in range(2):
        own = pltpu.roll(of(0, 0), 1, 1) if low == 0 else of(1, 0)
        ordered.append(jnp.where(head, own, of(1 - low, 0)))
        ordered += [of(1 - low, PIECE - v) for v in range(1, PIECE)]
    return jnp.concatenate(ordered, axis=0)


def make_response(received, response, fields):
    for w in range(4):
        blocks = [
            received[pl.ds((PIECE * v + low) * 6 + 2 + w, ROWS, stride=12), :]
            for low in range(2)
            for v in range(PIECE)
        ]
        word = swap_blocks(jnp.stack(blocks) if w < 2 else mirrored_blocks(blocks))
        for low in range(2):
            for v in range(PIECE):
                fields[w, pl.ds(LANES * low + v, ROWS, stride=PIECE), :] = word[PIECE * low + v]
    scale = f32(0.5 / (NX * NY))
    direct, mirror = decode(fields[0], fields[1]), decode(fields[2], fields[3])
    for f in range(4):
        response[f] = (direct[f] + mirror[f] if f % 2 == 0 else direct[f] - mirror[f]) * scale


def exchange(sent, axis, count):
    width = sent.size // count
    shape = (count, 1, width) if width == 6 * LANES else (count, width // LANES, LANES)
    return lax.all_to_all(
        sent.reshape(shape), axis, split_axis=0, concat_axis=0, tiled=True
    ).reshape(sent.shape)


def on_device(sky_image, observed, noise_weight, basis_tiles, intersection, counts, transfer):
    tables = {name: jnp.asarray(value) for name, value in make_tables().items()}
    band, column = lax.axis_index("sy"), lax.axis_index("sx")
    zero = jnp.zeros((), jnp.int32)
    wanted = lax.dynamic_slice(
        intersection, (2 * band + column // PIECE, zero, zero), (1, SHORT, 4)
    ).reshape(SHORT * 4) - band * LANES

    parts = exchange(
        run(
            pack_inputs,
            shaped(SHORT, TILE_ROWS + 6 * ROWS, LANES, dtype=jnp.bfloat16),
            basis_tiles,
            counts.reshape(2),
            sky_image,
            observed,
            noise_weight,
            far=5,
            scratch=[
                pltpu.VMEM(basis_tiles.shape, basis_tiles.dtype),
                pltpu.SMEM((2,), jnp.int32),
            ]
            + [pltpu.VMEM(sky_image.shape, f32)] * 3
            + [
                pltpu.VMEM((SHORT, TILE_ROWS + 6 * ROWS, LANES), jnp.bfloat16),
                pltpu.SemaphoreType.DMA((5,)),
                pltpu.SemaphoreType.DMA((4,)),
            ],
        ),
        "sx",
        SHORT,
    )
    special = jnp.where(band * SHORT + column < PIECE, 1, 0).astype(jnp.int32).reshape(1)
    spread = run(
        pack_transfer,
        shaped(DEVICES * 6, LANES, dtype=jnp.int32),
        special,
        transfer,
        tables["flips"],
        scalars=1,
        scratch=[pltpu.VMEM((8, DEVICES, LANES), f32)],
    )
    work = [pltpu.VMEM((DEVICES, 2 * LANES), f32)]
    sent, coef, pixels, top, bottom = run(
        first_rows,
        [
            shaped(DEVICES * 6, LANES, dtype=jnp.int32),
            shaped(4, SHORT, ROWS, LANES),
            shaped(SHORT, ROWS, LANES),
            shaped(SHORT, LANES),
            shaped(SHORT, LANES),
        ],
        wanted,
        parts,
        spread,
        tables["turn_x"],
        tables["x_forward"],
        scalars=1,
        scratch=[pltpu.VMEM((SHORT * TILE_ROWS, LANES), f32)] + work,
    )
    received = exchange(sent, EVERY, DEVICES)

    ahead = [(i, (i + 1) % DEVICES) for i in range(DEVICES)]
    behind = [(target, source) for source, target in ahead]
    above = lax.ppermute(bottom, EVERY, ahead)
    below = lax.ppermute(top, EVERY, behind)
    flow = run(variation, shaped(SHORT, ROWS, LANES), pixels, above, below)
    y_tables = [tables[name] for name in ("y_long", "turn_y", "y_forward", "y_inverse")]
    x_tables = [tables[name] for name in ("turn_x", "x_forward", "x_inverse")]
    sent, response = run(
        middle_lines,
        [shaped(DEVICES, LANES, dtype=jnp.int32), shaped(4, DEVICES, LANES)],
        received,
        *y_tables,
        scratch=[pltpu.VMEM((4, DEVICES, LANES), jnp.int32)],
    )
    received = exchange(sent, EVERY, DEVICES)
    sent, residual = run(
        middle_rows,
        [shaped(DEVICES, LANES, dtype=jnp.int32), shaped(SHORT, ROWS, LANES)],
        received,
        parts,
        *x_tables,
        scratch=work,
    )
    received = exchange(sent, EVERY, DEVICES)
    sent = run(
        last_lines, shaped(DEVICES * 2, LANES, dtype=jnp.int32), received, response, *y_tables
    )
    received = exchange(sent, EVERY, DEVICES)
    sent = run(
        last_rows,
        shaped(SHORT, 2 * ROWS, LANES),
        received,
        coef,
        residual,
        flow,
        tables["turn_x"],
        tables["x_inverse"],
        scratch=work,
    )
    blocks = exchange(sent, "sx", SHORT)
    gradient = blocks[:, :ROWS, :].reshape(SHORT * ROWS, LANES)
    residual = blocks[:, ROWS:, :].reshape(SHORT * ROWS, LANES)
    return (residual, gradient)


def solution(mesh):
    placed = (
        P("sy", "sx"),
        P("sy", "sx"),
        P("sy", "sx"),
        P(("sy", "sx"), None, None),
        P(),
        P("sy", "sx"),
        P(None, None, ("sy", "sx"), None),
    )
    return jax.shard_map(
        on_device,
        mesh=mesh,
        in_specs=placed,
        out_specs=(P("sy", "sx"), P("sy", "sx")),
        check_vma=False,
    )
```
